32 devices in a mesh: gx: 4 (over y, x), gy: 4 (over z), gz: 2 (over core).
Axes of the slice: x: 2, y: 2, z: 4, core: 2. Of those that a mesh axis runs over, the one named last changes fastest.
Arguments:
- populations: float32 [19, 32, 32, 512], P(None, 'gx', 'gz', 'gy'), may hold values from 0.005 to 0.6, as said below
- link_cell: int32 [4, 2, 4, 1024], P('gx', 'gz', 'gy'), may hold values from 0 to 16383, as said below
- link_dir: int32 [4, 2, 4, 1024], P('gx', 'gz', 'gy'), may hold values from 0 to 18, as said below
- link_slot: int32 [4, 2, 4, 1024], P('gx', 'gz', 'gy'), may hold values from 0 to 127, as said below
- link_arm: float32 [3, 4, 2, 4, 1024], P(None, 'gx', 'gz', 'gy'), may hold values from -6 to 6
- brick_bodies: int32 [4, 2, 4, 128], P('gx', 'gz', 'gy'), may hold values from 0 to 2047, as said below
- body_pos: float32 [3, 2048], P(None, ('gx', 'gy')), may hold values from -1 to 1
- body_quat: float32 [4, 2048], P(None, ('gx', 'gy')), may hold values from -1 to 1, as said below
- body_vel: float32 [3, 2048], P(None, ('gx', 'gy')), may hold values from -0.4 to 0.4
- body_spin: float32 [3, 2048], P(None, ('gx', 'gy')), may hold values from -0.4 to 0.4
- inv_mass: float32 [2048], P(('gx', 'gy')), may hold values from 0.5 to 4
- inv_inertia: float32 [3, 2048], P(None, ('gx', 'gy')), may hold values from 0.2 to 2
Outputs:
- next_populations: float32 [19, 32, 32, 512], P(None, 'gx', 'gz', 'gy')
- body_next: float32 [13, 2048], P(None, ('gx', 'gy'))
The draws below stay inside these ranges and needn't reach their ends.
Inputs may be any that keep to these rules, and one draw needn't show every extreme that they name: `populations`: every entry is positive, and the density (sum over the 19 directions) at every cell lies between 0.5 and 1.6. `link_cell`: within a brick all entries name different cells. `link_dir`: within a brick the used entries (direction 1 to 18) come first, unused ones have direction 0; some brick uses all 1024 entries in every draw. `link_slot`: unused entries hold 0. `brick_bodies`: each brick lists 128 different bodies; owner k holds bodies k*128 to (k+1)*128 - 1; a brick lists at most 16 bodies of one owner, and exactly 16 of some owner in every brick. `body_quat`: unit quaternions.
All inputs are finite; a program needn't handle non-finite values.
Results may differ from the reference program's by a relative error of at most 0.00013.
Values sent between devices are 32-bit elements; how exact they have to be, the bound alone decides.
A program may use at most 64 MiB of HBM per device.

```python
import math
import jax
import jax.numpy as jnp
import numpy as np
from jax import lax

CX = 8
CZ = 16
CY = 128
SLOTS = 128
BODY_OWN = 128
LINKS = 1024
NB = 2048
CAP = 16
NX = 32
NZ = 32
NY = 512
N_GX = 4
N_GY = 4
N_GZ = 2


lattice_vel = np.array([[0, 0, 0], [1, 0, 0], [-1, 0, 0], [0, 1, 0], [0, -1, 0], [0, 0, 1], [0, 0, -1], [1, 1, 0], [-1, -1, 0], [1, -1, 0], [-1, 1, 0], [1, 0, 1], [-1, 0, -1], [1, 0, -1], [-1, 0, 1], [0, 1, 1], [0, -1, -1], [0, 1, -1], [0, -1, 1]])


lattice_wt = np.array([1.0 / 3.0] + [1.0 / 18.0] * 6 + [1.0 / 36.0] * 12)


def draw_populations(key, part):
    key_dens, key_flow, key_noise = jax.random.split(jax.random.fold_in(key, 3), 3)
    shape = (NX, NZ, NY)
    density = jax.random.uniform(key_dens, shape, jnp.float32, 0.9, 1.1)
    flows = jnp.clip(0.05 * jax.random.normal(key_flow, (3,) + shape, jnp.float32), -0.15, 0.15)
    noise = jnp.clip(0.1 * jax.random.normal(key_noise, (19,) + shape, jnp.float32), -0.3, 0.3)
    speed_sq = flows[0] * flows[0] + flows[1] * flows[1] + flows[2] * flows[2]
    result = []
    for direction in range(19):
        proj = float(lattice_vel[direction, 0]) * flows[0] + float(lattice_vel[direction, 1]) * flows[1] + float(lattice_vel[direction, 2]) * flows[2]
        equil = float(lattice_wt[direction]) * density * (1.0 + 3.0 * proj + 4.5 * proj * proj - 1.5 * speed_sq)
        result.append(equil * (1.0 + noise[direction]))
    return jnp.stack(result).astype(jnp.float32)


def link_fields(key):
    base = jax.random.fold_in(key, 7)
    key_cell, key_perm, key_dir, key_slot, key_count = jax.random.split(base, 5)
    bricks = N_GX * N_GZ * N_GY
    cells = CX * CZ * CY
    stride = cells // LINKS
    entry = jnp.arange(LINKS, dtype=jnp.int32)
    offsets = jax.random.randint(key_cell, (bricks, LINKS), 0, stride, dtype=jnp.int32)
    cell_idx = entry[None, :] * stride + offsets
    scores = jax.random.randint(key_perm, (bricks, LINKS), 0, 2 ** 18, dtype=jnp.int32) * LINKS + entry[None, :]
    order = jnp.argsort(scores, axis=1)
    cell_idx = jnp.take_along_axis(cell_idx, order, axis=1)
    layer_z = jnp.arange(bricks, dtype=jnp.int32) // N_GY % N_GZ
    counts = jax.random.randint(key_count, (bricks,), LINKS // 4, LINKS // 2 + 1, dtype=jnp.int32)
    counts = jnp.where(layer_z == 0, LINKS, counts)
    live = entry[None, :] < counts[:, None]
    dirs = jnp.where(live, jax.random.randint(key_dir, (bricks, LINKS), 1, 19, dtype=jnp.int32), 0)
    slots = jnp.where(live, jax.random.randint(key_slot, (bricks, LINKS), 0, SLOTS, dtype=jnp.int32), 0)
    shape = (N_GX, N_GZ, N_GY, LINKS)
    return (cell_idx.reshape(shape), dirs.reshape(shape), slots.reshape(shape))


def draw_link_cell(key, part):
    return link_fields(key)[0]


def draw_link_dir(key, part):
    return link_fields(key)[1]


def draw_link_slot(key, part):
    return link_fields(key)[2]


def draw_brick_bodies(key, part):
    key_perm, key_pick, key_offs = jax.random.split(jax.random.fold_in(key, 11), 3)
    bricks = N_GX * N_GZ * N_GY
    owners = N_GX * N_GY
    total = owners * CAP
    entry = jnp.arange(total, dtype=jnp.int32)
    scores = jax.random.randint(key_perm, (bricks, total), 0, 2 ** 18, dtype=jnp.int32) * total + entry[None, :]
    chosen = jax.random.randint(key_pick, (bricks,), 0, owners, dtype=jnp.int32)
    scores = jnp.where((entry // CAP)[None, :] == chosen[:, None], -total + (entry % CAP)[None, :], scores)
    order = jnp.argsort(scores, axis=1)[:, :SLOTS]
    owner_of = order // CAP
    copy_of = order % CAP
    offsets = jax.random.randint(key_offs, (bricks, owners), 0, BODY_OWN, dtype=jnp.int32)
    base_off = jnp.take_along_axis(offsets, owner_of, axis=1)
    local = (base_off + copy_of * (BODY_OWN // CAP)) % BODY_OWN
    return (owner_of * BODY_OWN + local).reshape(N_GX, N_GZ, N_GY, SLOTS)


def draw_body_quat(key, part):
    base = jax.random.fold_in(key, 13)
    raw = jax.random.normal(base, (4, NB), jnp.float32)
    return (raw / jnp.sqrt(jnp.sum(raw * raw, 0, keepdims=True) + 1e-12)).astype(jnp.float32)


def shard_levels(key, dims, pieces, low, largest):
    def one(dim, parts):
        steps = jax.random.uniform(jax.random.fold_in(jax.random.fold_in(key, 6), dim), (parts,), jnp.float32, low / len(pieces), largest / len(pieces))
        return jnp.repeat(jnp.exp(steps), dims[dim] // parts).reshape((-1,) + (1,) * (len(dims) - dim - 1))

    factor_of = one(*pieces[0])
    for cut in pieces[1:]:
        factor_of = factor_of * one(*cut)
    return factor_of


def centred(rng, dims, scale, reach, cuts=(), kind=jnp.bfloat16):
    values = jax.random.normal(rng, dims, jnp.float32) * scale
    if len(cuts) > 0:
        values = shard_levels(rng, dims, cuts, -0.22, 0.18) * values
    return jnp.clip(values, min=-reach, max=reach).astype(kind)


def setup_inputs(seed: int = 0) -> dict:
    arg_keys = jax.random.split(jax.random.key(seed), 13)
    populations = draw_populations(jax.random.fold_in(arg_keys[12], 71), 0)
    link_cell = draw_link_cell(jax.random.fold_in(arg_keys[12], 71), 0)
    link_dir = draw_link_dir(jax.random.fold_in(arg_keys[12], 71), 0)
    link_slot = draw_link_slot(jax.random.fold_in(arg_keys[12], 71), 0)
    link_arm = centred(arg_keys[4], (3, N_GX, N_GZ, N_GY, LINKS), 2.0, 6.0, ((1, 4), (2, 2), (3, 4)), jnp.float32)
    brick_bodies = draw_brick_bodies(jax.random.fold_in(arg_keys[12], 71), 0)
    body_pos = jnp.clip(jax.random.uniform(arg_keys[6], (3, NB), jnp.float32, -1.0, 1.0) * shard_levels(arg_keys[6], (3, NB), ((1, 16),), -0.4, 0.0), -1.0, 1.0)
    body_quat = draw_body_quat(jax.random.fold_in(arg_keys[12], 71), 0)
    body_vel = centred(arg_keys[8], (3, NB), 0.1, 0.4, ((1, 16),), jnp.float32)
    body_spin = centred(arg_keys[9], (3, NB), 0.1, 0.4, ((1, 16),), jnp.float32)
    inv_mass = jnp.clip(jnp.exp(math.log(4.0) - 2.0794415 * jax.random.uniform(arg_keys[10], (NB,), jnp.float32) ** shard_levels(arg_keys[10], (NB,), ((0, 16),), -0.2, 0.2)), 0.5, 4.0)
    inv_inertia = jnp.clip(jnp.exp(math.log(2.0) - 2.3025851 * jax.random.uniform(arg_keys[11], (3, NB), jnp.float32) ** shard_levels(arg_keys[11], (3, NB), ((1, 16),), -0.2, 0.2)), 0.2, 2.0)
    return dict(populations=populations, link_cell=link_cell, link_dir=link_dir, link_slot=link_slot, link_arm=link_arm, brick_bodies=brick_bodies, body_pos=body_pos, body_quat=body_quat, body_vel=body_vel, body_spin=body_spin, inv_mass=inv_mass, inv_inertia=inv_inertia)


lattice_vel = np.array([[0, 0, 0], [1, 0, 0], [-1, 0, 0], [0, 1, 0], [0, -1, 0], [0, 0, 1], [0, 0, -1], [1, 1, 0], [-1, -1, 0], [1, -1, 0], [-1, 1, 0], [1, 0, 1], [-1, 0, -1], [1, 0, -1], [-1, 0, 1], [0, 1, 1], [0, -1, -1], [0, 1, -1], [0, -1, 1]])
lattice_wt = np.array([1.0 / 3.0] + [1.0 / 18.0] * 6 + [1.0 / 36.0] * 12)
opposite_dir = np.array([0, 2, 1, 4, 3, 6, 5, 8, 7, 10, 9, 12, 11, 14, 13, 16, 15, 18, 17])
omega_relax = 1.25
grav_accel = 0.02

def collide(populations):
    density = populations[0]
    for direction in range(1, 19):
        density = density + populations[direction]
    flows = []
    for comp_index in range(3):
        total = jnp.zeros_like(density)
        for direction in range(19):
            if lattice_vel[direction, comp_index] == 1:
                total = total + populations[direction]
            elif lattice_vel[direction, comp_index] == -1:
                total = total - populations[direction]
        flows.append(total / density)
    speed_sq = flows[0] * flows[0] + flows[1] * flows[1] + flows[2] * flows[2]
    relaxed = []
    for direction in range(19):
        proj = float(lattice_vel[direction, 0]) * flows[0] + float(lattice_vel[direction, 1]) * flows[1] + float(lattice_vel[direction, 2]) * flows[2]
        equil = float(lattice_wt[direction]) * density * (1.0 + 3.0 * proj + 4.5 * proj * proj - 1.5 * speed_sq)
        relaxed.append(populations[direction] - omega_relax * (populations[direction] - equil))
    return jnp.stack(relaxed)

def link_terms(post_out, link_dirs, arm, motion_at):
    iota_dir = jnp.arange(19, dtype=jnp.int32)
    onehot = (link_dirs[None, :] == iota_dir[:, None]).astype(jnp.float32)
    table = jnp.asarray(np.concatenate([lattice_vel.T, lattice_wt[None, :]], 0), jnp.float32)
    coeffs = jnp.dot(table, onehot, precision=lax.Precision.HIGHEST)
    vel_x, vel_y, vel_z = (coeffs[0], coeffs[1], coeffs[2])
    weight = coeffs[3]
    opp_table = jnp.asarray(opposite_dir, jnp.int32)
    opp_dir = lax.optimization_barrier(jnp.sum(opp_table[:, None] * (link_dirs[None, :] == iota_dir[:, None]).astype(jnp.int32), 0))
    wall_x = motion_at[0] + motion_at[4] * arm[2] - motion_at[5] * arm[1]
    wall_y = motion_at[1] + motion_at[5] * arm[0] - motion_at[3] * arm[2]
    wall_z = motion_at[2] + motion_at[3] * arm[1] - motion_at[4] * arm[0]
    proj = vel_x * wall_x + vel_y * wall_y + vel_z * wall_z
    bounce = post_out - 6.0 * weight * proj
    live = (link_dirs > 0).astype(jnp.float32)
    exchanged = (post_out + bounce) * live
    force_x, force_y, force_z = (vel_x * exchanged, vel_y * exchanged, vel_z * exchanged)
    torque_x = arm[1] * force_z - arm[2] * force_y
    torque_y = arm[2] * force_x - arm[0] * force_z
    torque_z = arm[0] * force_y - arm[1] * force_x
    loads = jnp.stack([force_x, force_y, force_z, torque_x, torque_y, torque_z])
    return (bounce, live, opp_dir, loads)

def integrate(body_pos, body_quat, body_vel, body_spin, inv_mass, inv_inertia, load):
    gravity = jnp.asarray(np.array([0.0, 0.0, -grav_accel]), jnp.float32)[:, None]
    velocity = body_vel + inv_mass[None, :] * load[0:3] + gravity
    quat_w, quat_x, quat_y, quat_z = (body_quat[0], body_quat[1], body_quat[2], body_quat[3])
    rotation = [[1.0 - 2.0 * (quat_y * quat_y + quat_z * quat_z), 2.0 * (quat_x * quat_y - quat_w * quat_z), 2.0 * (quat_x * quat_z + quat_w * quat_y)], [2.0 * (quat_x * quat_y + quat_w * quat_z), 1.0 - 2.0 * (quat_x * quat_x + quat_z * quat_z), 2.0 * (quat_y * quat_z - quat_w * quat_x)], [2.0 * (quat_x * quat_z - quat_w * quat_y), 2.0 * (quat_y * quat_z + quat_w * quat_x), 1.0 - 2.0 * (quat_x * quat_x + quat_y * quat_y)]]
    torque = load[3:6]
    frame_torque = [rotation[0][col] * torque[0] + rotation[1][col] * torque[1] + rotation[2][col] * torque[2] for col in range(3)]
    frame_accel = [inv_inertia[col] * frame_torque[col] for col in range(3)]
    accel = [rotation[row][0] * frame_accel[0] + rotation[row][1] * frame_accel[1] + rotation[row][2] * frame_accel[2] for row in range(3)]
    spin = body_spin + jnp.stack(accel)
    position = body_pos + velocity
    spin_x, spin_y, spin_z = (spin[0], spin[1], spin[2])
    delta_w = -(spin_x * quat_x + spin_y * quat_y + spin_z * quat_z)
    delta_x = spin_x * quat_w + spin_y * quat_z - spin_z * quat_y
    delta_y = spin_y * quat_w + spin_z * quat_x - spin_x * quat_z
    delta_z = spin_z * quat_w + spin_x * quat_y - spin_y * quat_x
    scale = lax.rsqrt(1.0 + 0.25 * (spin_x * spin_x + spin_y * spin_y + spin_z * spin_z))
    quat = jnp.stack([quat_w + 0.5 * delta_w, quat_x + 0.5 * delta_x, quat_y + 0.5 * delta_y, quat_z + 0.5 * delta_z]) * scale[None, :]
    return jnp.concatenate([position, quat, velocity, spin], 0)

def reference(populations, link_cell, link_dir, link_slot, link_arm, brick_bodies, body_pos, body_quat, body_vel, body_spin, inv_mass, inv_inertia):
    relaxed = collide(populations)
    read = jnp.stack([jnp.roll(relaxed[direction], (int(lattice_vel[direction, 0]), int(lattice_vel[direction, 2]), int(lattice_vel[direction, 1])), axis=(0, 1, 2)) for direction in range(19)])
    brick_x = jnp.arange(N_GX, dtype=jnp.int32)[:, None, None, None]
    brick_z = jnp.arange(N_GZ, dtype=jnp.int32)[None, :, None, None]
    brick_y = jnp.arange(N_GY, dtype=jnp.int32)[None, None, :, None]
    glob_x = (brick_x * CX + link_cell // (CZ * CY)).reshape(-1)
    glob_z = (brick_z * CZ + link_cell // CY % CZ).reshape(-1)
    glob_y = (brick_y * CY + link_cell % CY).reshape(-1)
    link_dirs = link_dir.reshape(-1)
    link_bodies = jnp.take_along_axis(brick_bodies, link_slot, axis=3).reshape(-1)
    arm = link_arm.reshape(3, -1)
    motion_at = jnp.concatenate([body_vel, body_spin], 0)[:, link_bodies]
    post_out = relaxed[link_dirs, glob_x, glob_z, glob_y]
    bounce, live, opp_dir, loads = link_terms(post_out, link_dirs, arm, motion_at)
    current = read[opp_dir, glob_x, glob_z, glob_y]
    next_populations = read.at[opp_dir, glob_x, glob_z, glob_y].add(live * (bounce - current))
    load = jax.ops.segment_sum(loads.T, link_bodies, num_segments=NB).T
    return (next_populations, integrate(body_pos, body_quat, body_vel, body_spin, inv_mass, inv_inertia, load))
```

```python
import functools

import jax
import jax.numpy as jnp
import numpy as np
from jax import lax
from jax.experimental import pallas as pl
from jax.experimental.pallas import tpu as pltpu
from jax.sharding import PartitionSpec as P

VEL = [
    (0, 0, 0), (1, 0, 0), (-1, 0, 0), (0, 1, 0), (0, -1, 0), (0, 0, 1), (0, 0, -1),
    (1, 1, 0), (-1, -1, 0), (1, -1, 0), (-1, 1, 0), (1, 0, 1), (-1, 0, -1), (1, 0, -1),
    (-1, 0, 1), (0, 1, 1), (0, -1, -1), (0, 1, -1), (0, -1, 1),
]
WT = [1.0 / 3.0] + [1.0 / 18.0] * 6 + [1.0 / 36.0] * 12
OPP = [0, 2, 1, 4, 3, 6, 5, 8, 7, 10, 9, 12, 11, 14, 13, 16, 15, 18, 17]
OMEGA = 1.25
GRAV = 0.02
F32 = jnp.float32
BF16 = jnp.bfloat16


def dirs_of(comp, sign):
    return [d for d in range(19) if VEL[d][comp] == sign]


XD = (dirs_of(0, 1), dirs_of(0, -1))
YD = (dirs_of(1, 1), dirs_of(1, -1))
ZD = (dirs_of(2, 1), dirs_of(2, -1))
XZD = tuple([d for d in XD[s] if VEL[d][2] != 0] for s in range(2))


def split3(v):
    hi = v.astype(BF16).astype(F32)
    rest = v - hi
    mid = rest.astype(BF16).astype(F32)
    return hi, mid, rest - mid


def dot(a, b, ca, cb):
    return lax.dot_general(a, b, (((ca,), (cb,)), ((), ())), preferred_element_type=F32)


def stacked(v):
    return jnp.concatenate(split3(v), 0).astype(BF16)


def unstacked(v):
    k = v.shape[0] // 3
    return v[0:k] + v[k : 2 * k] + v[2 * k : 3 * k]


def kernel(
    sizes,
    pop, lcell, ldir, lslot, larm, bb_ref, bpos, bquat, bvel, bspin, imass, iinert,
    nxt, bnext,
    relaxed, sendx, xin, sendz, zin, sende, ein, sendy, yin, yflat, ycols,
    dmap, wmap, motion_own, motion_all, tiles, force_all, half, half_in,
    hs, hr, ms, mr, fs, fr, cs, cr,
):
    ngx, ngy = sizes
    owners = ngx * ngy
    span_x, span_z, span_y = pop.shape[1:]
    cells = span_x * span_z
    links = lcell.shape[-1]
    body_own = bvel.shape[1]
    slots = bb_ref.shape[-1]
    a, b, e = lax.axis_index("gx"), lax.axis_index("gy"), lax.axis_index("gz")
    me = a * ngy + b
    ap, am = lax.rem(a + 1, ngx), lax.rem(a + ngx - 1, ngx)
    bp, bm = lax.rem(b + 1, ngy), lax.rem(b + ngy - 1, ngy)
    oe = 1 - e

    def dev(x, y, z):
        return {"gx": x, "gy": y, "gz": z}

    def peer_of(offset):
        p = lax.rem(me + offset, owners)
        return p, dev(p // ngy, lax.rem(p, ngy), e)

    unroll = owners <= 16

    def loop(lo, hi, body):
        if unroll:
            for i in range(lo, hi):
                body(i)
        else:
            pl.loop(lo, hi)(body)

    barrier = pltpu.get_barrier_semaphore()

    def greet(o):
        pl.semaphore_signal(barrier, inc=1, device_id=peer_of(o)[1], device_id_type=pl.DeviceIdType.MESH)

    loop(1, owners, greet)
    others = [dev(a, b, oe), dev(ap, b, oe), dev(am, b, oe), dev(a, bp, oe), dev(a, bm, oe)]
    for t in others:
        pl.semaphore_signal(barrier, inc=1, device_id=t, device_id_type=pl.DeviceIdType.MESH)

    motion_own[...] = jnp.concatenate(
        [bvel[...], bspin[...], jnp.zeros((2, body_own), F32)], 0
    )
    motion_all[me] = motion_own[...]

    for x in range(span_x):
        for z in range(0, span_z, 8):
            f = [pop[d, x, z : z + 8, :] for d in range(19)]
            rho = f[0]
            for d in range(1, 19):
                rho = rho + f[d]
            inv = 1.0 / rho
            u = []
            for c in range(3):
                pos, neg = dirs_of(c, 1), dirs_of(c, -1)
                tot = f[pos[0]] - f[neg[0]]
                for p, q in zip(pos[1:], neg[1:]):
                    tot = tot + (f[p] - f[q])
                u.append(tot * inv)
            usq = 1.0 - 1.5 * (u[0] * u[0] + u[1] * u[1] + u[2] * u[2])
            rows = pl.ds(x * span_z + z, 8)
            keep = 1.0 - OMEGA
            relaxed[0, rows, :] = keep * f[0] + (OMEGA * WT[0]) * rho * usq
            for d in range(1, 19, 2):
                terms = [u[c] if VEL[d][c] > 0 else -u[c] for c in range(3) if VEL[d][c]]
                proj = terms[0] if len(terms) == 1 else terms[0] + terms[1]
                scale = (OMEGA * WT[d]) * rho
                even = scale * (usq + 4.5 * proj * proj)
                odd = scale * (3.0 * proj)
                relaxed[d, rows, :] = keep * f[d] + (even + odd)
                relaxed[d + 1, rows, :] = keep * f[d + 1] + (even - odd)

    for s in range(2):
        xe = (span_x - 1) if s == 0 else 0
        ze = (span_z - 1) if s == 0 else 0
        for j, d in enumerate(XD[s]):
            sendx[s, j] = relaxed[d, xe * span_z : (xe + 1) * span_z, :]
        for j, d in enumerate(ZD[s]):
            for x in range(span_x):
                r = x * span_z + ze
                sendz[s, j, x : x + 1, :] = relaxed[d, r : r + 1, :]
        sende[s] = jnp.zeros(sende.shape[1:], F32)
        for j, d in enumerate(XZD[s]):
            r = xe * span_z + ((span_z - 1) if VEL[d][2] > 0 else 0)
            sende[s, j : j + 1, :] = relaxed[d, r : r + 1, :]
    lane = lax.broadcasted_iota(jnp.int32, (cells, span_y), 1)
    pack = jnp.zeros((cells, span_y), F32)
    for s in range(2):
        ye = (span_y - 1) if s == 0 else 0
        for j, d in enumerate(YD[s]):
            pack = jnp.where(lane == 8 * s + j, relaxed[d, :, ye : ye + 1], pack)
    pack_t = pack.T
    for s in range(2):
        sendy[s] = pack_t[8 * s : 8 * s + 8, :]

    pl.semaphore_wait(barrier, owners - 1 + len(others))

    def motion_copy(o, slot):
        return pltpu.make_async_remote_copy(
            src_ref=motion_own, dst_ref=motion_all.at[slot], send_sem=ms.at[o], recv_sem=mr.at[slot],
            device_id=peer_of(o)[1], device_id_type=pl.DeviceIdType.MESH,
        )

    loop(1, owners, lambda o: motion_copy(o, me).start())

    halo = []

    def rim(src, dst, target):
        k = len(halo)
        c = pltpu.make_async_remote_copy(
            src_ref=src, dst_ref=dst, send_sem=hs.at[k], recv_sem=hr.at[k],
            device_id=target, device_id_type=pl.DeviceIdType.MESH,
        )
        c.start()
        halo.append(c)

    for s in range(2):
        xt, yt = (ap, bp) if s == 0 else (am, bm)
        rim(sendx.at[s], xin.at[s], dev(xt, b, e))
        rim(sende.at[s], ein.at[s], dev(xt, b, oe))
        rim(sendy.at[s], yin.at[s, 0], dev(a, yt, e))
        rim(sendy.at[s], yin.at[s, 1], dev(ap, yt, e))
        rim(sendy.at[s], yin.at[s, 2], dev(am, yt, e))
        rim(sendy.at[s], yin.at[s, 3], dev(a, yt, oe))
    rim(sendz, zin, dev(a, b, oe))

    cell = lcell[0, 0]
    dirs = ldir[0, 0]
    row_of = cell // span_y
    lane_of = cell - row_of * span_y
    dirs_f = dirs.astype(F32)
    iota_c = lax.broadcasted_iota(jnp.int32, (cells, links), 0)
    iota_y = lax.broadcasted_iota(jnp.int32, (span_y, links), 0)
    row_t = jnp.where(iota_c == row_of, 1.0, 0.0).astype(BF16)
    lane_mask = iota_y == lane_of
    dmap[...] = dot(row_t, jnp.where(lane_mask, dirs_f, 0.0).astype(BF16), 1, 1)
    dm = dmap[...]
    post_map = jnp.zeros((cells, span_y), F32)
    for d in range(1, 19):
        post_map = jnp.where(dm == float(d), relaxed[d], post_map)
    picked = None
    for part in split3(post_map):
        t = dot(part.astype(BF16), row_t, 0, 0)
        picked = t if picked is None else picked + t
    post = jnp.sum(jnp.where(lane_mask, picked, 0.0), axis=0, keepdims=True)
    iota_s = lax.broadcasted_iota(jnp.int32, (slots, links), 0)
    slot_t = jnp.where(iota_s == lslot[0, 0], 1.0, 0.0).astype(BF16)

    vel = []
    for c in range(3):
        v = jnp.zeros((1, links), F32)
        for d in range(1, 19):
            if VEL[d][c]:
                v = jnp.where(dirs == d, float(VEL[d][c]), v)
        vel.append(v)
    six_w = jnp.where(dirs > 6, 6.0 * WT[7], 6.0 * WT[1])

    def motion_wait(o):
        p, _ = peer_of(o)
        motion_copy(o, p).wait_recv()

    loop(1, owners, motion_wait)
    bodies = bb_ref[0, 0]
    iota_b = lax.broadcasted_iota(jnp.int32, (body_own, slots), 0)

    def owner_onehot(o):
        return jnp.where(iota_b == bodies - o * body_own, 1.0, 0.0).astype(BF16)

    def gather(o, acc):
        return acc + dot(stacked(motion_all[o]), owner_onehot(o), 1, 0)

    slot_motion = unstacked(
        lax.fori_loop(0, owners, gather, jnp.zeros((24, slots), F32), unroll=unroll)
    )
    m = unstacked(dot(stacked(slot_motion), slot_t, 1, 0))
    mv = [m[i : i + 1, :] for i in range(6)]
    arm = [larm[i, 0, 0] for i in range(3)]
    wall = [
        mv[0] + mv[4] * arm[2] - mv[5] * arm[1],
        mv[1] + mv[5] * arm[0] - mv[3] * arm[2],
        mv[2] + mv[3] * arm[1] - mv[4] * arm[0],
    ]
    drop = six_w * (vel[0] * wall[0] + vel[1] * wall[1] + vel[2] * wall[2])
    bounce = post - drop
    live = jnp.where(dirs > 0, 1.0, 0.0)
    exchanged = (post + bounce) * live
    force = [vel[c] * exchanged for c in range(3)]
    torque = [
        arm[1] * force[2] - arm[2] * force[1],
        arm[2] * force[0] - arm[0] * force[2],
        arm[0] * force[1] - arm[1] * force[0],
    ]
    loads = jnp.concatenate(force + torque + [jnp.zeros((2, links), F32)], 0)
    slot_load = unstacked(dot(stacked(loads), slot_t, 1, 1))
    slot_parts = stacked(slot_load)

    def spread(o):
        tiles[o] = unstacked(dot(slot_parts, owner_onehot(o), 1, 1))

    loop(0, owners, spread)

    def force_copy(o, src, slot):
        return pltpu.make_async_remote_copy(
            src_ref=tiles.at[src], dst_ref=force_all.at[slot], send_sem=fs.at[o], recv_sem=fr.at[slot],
            device_id=peer_of(o)[1], device_id_type=pl.DeviceIdType.MESH,
        )

    loop(1, owners, lambda o: force_copy(o, peer_of(o)[0], me).start())
    force_all[me] = tiles[me]

    wm = None
    for part in split3(drop):
        t = dot(row_t, jnp.where(lane_mask, part, 0.0).astype(BF16), 1, 1)
        wm = t if wm is None else wm + t
    wmap[...] = wm

    for c in halo:
        c.wait_recv()
    lane_c = lax.broadcasted_iota(jnp.int32, (8, cells), 1)
    z_c = lane_c - (lane_c // span_z) * span_z
    sub_c = lax.broadcasted_iota(jnp.int32, (8, cells), 0)
    both = []
    for s in range(2):
        t0, t1, t2, t3 = (yin[s, k] for k in range(4))
        out = t0
        for j, d in enumerate(YD[s]):
            cx, _, cz = VEL[d]
            if cx == 1:
                v = jnp.where(lane_c < span_z, pltpu.roll(t1, span_z, 1), pltpu.roll(t0, span_z, 1))
            elif cx == -1:
                v = jnp.where(
                    lane_c >= cells - span_z,
                    pltpu.roll(t2, cells - span_z, 1),
                    pltpu.roll(t0, cells - span_z, 1),
                )
            elif cz == 1:
                v = jnp.where(z_c == 0, pltpu.roll(t3, cells - span_z + 1, 1), pltpu.roll(t0, 1, 1))
            elif cz == -1:
                v = jnp.where(
                    z_c == span_z - 1, pltpu.roll(t3, span_z - 1, 1), pltpu.roll(t0, cells - 1, 1)
                )
            else:
                continue
            out = jnp.where(sub_c == j, v, out)
        both.append(out)
    both.append(jnp.zeros((span_y - 16, cells), F32))
    ycols[...] = jnp.concatenate(both, 0).T

    iz = lax.broadcasted_iota(jnp.int32, (span_z, span_y), 0)
    iy = lax.broadcasted_iota(jnp.int32, (span_z, span_y), 1)
    for x in range(span_x):
        rows = slice(x * span_z, (x + 1) * span_z)
        dm_x = dmap[rows, :]
        wm_x = wmap[rows, :]
        for i in range(19):
            cx, cy, cz = VEL[i]
            sx = x - cx
            inside = 0 <= sx < span_x
            if inside:
                v = relaxed[i, sx * span_z : (sx + 1) * span_z, :]
            else:
                s = 0 if cx > 0 else 1
                v = xin[s, XD[s].index(i)]
            if cz:
                s = 0 if cz > 0 else 1
                if inside:
                    edge = zin[s, ZD[s].index(i), sx : sx + 1, :]
                else:
                    sxx = 0 if cx > 0 else 1
                    j = XZD[sxx].index(i)
                    edge = ein[sxx, j : j + 1, :]
                v = pltpu.roll(v, 1 if cz > 0 else span_z - 1, 0)
                v = jnp.where(iz == (0 if cz > 0 else span_z - 1), edge, v)
            if cy:
                s = 0 if cy > 0 else 1
                j = 8 * s + YD[s].index(i)
                v = pltpu.roll(v, 1 if cy > 0 else span_y - 1, 1)
                v = jnp.where(iy == (0 if cy > 0 else span_y - 1), ycols[rows, j : j + 1], v)
            if i:
                d = OPP[i]
                v = jnp.where(dm_x == float(d), relaxed[d, rows, :] - wm_x, v)
            nxt[i, x] = v

    def force_wait(o):
        p, _ = peer_of(o)
        force_copy(o, p, p).wait_recv()

    loop(1, owners, force_wait)
    half[...] = lax.fori_loop(
        0, owners, lambda o, acc: acc + force_all[o], jnp.zeros(half.shape, F32), unroll=unroll
    )
    swap = pltpu.make_async_remote_copy(
        src_ref=half, dst_ref=half_in, send_sem=cs, recv_sem=cr,
        device_id=dev(a, b, oe), device_id_type=pl.DeviceIdType.MESH,
    )
    swap.start()

    def sent(o):
        motion_copy(o, me).wait_send()
        force_copy(o, peer_of(o)[0], me).wait_send()

    loop(1, owners, sent)
    for c in halo:
        c.wait_send()
    swap.wait()
    load = half[...] + half_in[...]
    f = [load[i : i + 1, :] for i in range(6)]
    pos = [bpos[i : i + 1, :] for i in range(3)]
    qw, qx, qy, qz = (bquat[i : i + 1, :] for i in range(4))
    velo = [bvel[i : i + 1, :] + imass[...] * f[i] for i in range(3)]
    velo[2] = velo[2] - GRAV
    rot = [
        [1.0 - 2.0 * (qy * qy + qz * qz), 2.0 * (qx * qy - qw * qz), 2.0 * (qx * qz + qw * qy)],
        [2.0 * (qx * qy + qw * qz), 1.0 - 2.0 * (qx * qx + qz * qz), 2.0 * (qy * qz - qw * qx)],
        [2.0 * (qx * qz - qw * qy), 2.0 * (qy * qz + qw * qx), 1.0 - 2.0 * (qx * qx + qy * qy)],
    ]
    tq = f[3:6]
    acc = [
        iinert[c : c + 1, :] * (rot[0][c] * tq[0] + rot[1][c] * tq[1] + rot[2][c] * tq[2])
        for c in range(3)
    ]
    spin = [
        bspin[r : r + 1, :] + (rot[r][0] * acc[0] + rot[r][1] * acc[1] + rot[r][2] * acc[2])
        for r in range(3)
    ]
    sx, sy, sz = spin
    dq = [
        -(sx * qx + sy * qy + sz * qz),
        sx * qw + sy * qz - sz * qy,
        sy * qw + sz * qx - sx * qz,
        sz * qw + sx * qy - sy * qx,
    ]
    scale = lax.rsqrt(1.0 + 0.25 * (sx * sx + sy * sy + sz * sz))
    quat = [(q + 0.5 * k) * scale for q, k in zip((qw, qx, qy, qz), dq)]
    result = [pos[i] + velo[i] for i in range(3)] + quat + velo + spin
    for i, v in enumerate(result):
        bnext[i : i + 1, :] = v


def shards(sizes, *args):
    pop = args[0]
    span_x, span_z, span_y = pop.shape[1:]
    cells = span_x * span_z
    body_own = args[6].shape[1]
    owners = sizes[0] * sizes[1]
    args = list(args)
    args[10] = args[10].reshape(1, -1)
    vm = pl.BlockSpec(memory_space=pltpu.VMEM)
    dma = pltpu.SemaphoreType.DMA
    V = lambda *s: pltpu.VMEM(s, F32)
    return pl.pallas_call(
        functools.partial(kernel, sizes),
        out_shape=(
            jax.ShapeDtypeStruct(pop.shape, F32),
            jax.ShapeDtypeStruct((13, body_own), F32),
        ),
        in_specs=[vm] * len(args),
        out_specs=(vm, vm),
        scratch_shapes=[
            V(19, cells, span_y),
            V(2, 5, span_z, span_y), V(2, 5, span_z, span_y),
            V(2, 5, span_x, span_y), V(2, 5, span_x, span_y),
            V(2, 8, span_y), V(2, 8, span_y),
            V(2, 8, cells), V(2, 4, 8, cells),
            V(16, cells), V(cells, span_y),
            V(cells, span_y), V(cells, span_y),
            V(8, body_own), V(owners, 8, body_own),
            V(owners, 8, body_own), V(owners, 8, body_own),
            V(8, body_own), V(8, body_own),
            dma((13,)), dma((13,)),
            dma((owners,)), dma((owners,)),
            dma((owners,)), dma((owners,)),
            dma, dma,
        ],
        compiler_params=pltpu.CompilerParams(
            collective_id=0, has_side_effects=True, vmem_limit_bytes=48 * 1024 * 1024
        ),
        name="lattice_step",
    )(*args)


def solution(mesh):
    sizes = (mesh.shape["gx"], mesh.shape["gy"])
    link = P("gx", "gz", "gy", None)
    body = P(None, ("gx", "gy"))
    return jax.shard_map(
        functools.partial(shards, sizes),
        mesh=mesh,
        in_specs=(
            P(None, "gx", "gz", "gy"), link, link, link, P(None, "gx", "gz", "gy", None), link,
            body, body, body, body, P(("gx", "gy")), body,
        ),
        out_specs=(P(None, "gx", "gz", "gy"), body),
        check_vma=False,
    )
```

```python
import functools

import jax
import jax.numpy as jnp
import numpy as np
from jax import lax
from jax.experimental import pallas as pl
from jax.experimental.pallas import tpu as pltpu
from jax.sharding import PartitionSpec as P

VEL = [
    (0, 0, 0), (1, 0, 0), (-1, 0, 0), (0, 1, 0), (0, -1, 0), (0, 0, 1), (0, 0, -1),
    (1, 1, 0), (-1, -1, 0), (1, -1, 0), (-1, 1, 0), (1, 0, 1), (-1, 0, -1), (1, 0, -1),
    (-1, 0, 1), (0, 1, 1), (0, -1, -1), (0, 1, -1), (0, -1, 1),
]
WT = [1.0 / 3.0] + [1.0 / 18.0] * 6 + [1.0 / 36.0] * 12
OPP = [0, 2, 1, 4, 3, 6, 5, 8, 7, 10, 9, 12, 11, 14, 13, 16, 15, 18, 17]
OMEGA = 1.25
POP_CHUNKS = 2
K1_VMEM = 48 * 1024 * 1024
K2_VMEM = 1024 * 1024
GRAV = 0.02
F32 = jnp.float32
BF16 = jnp.bfloat16


def dirs_of(comp, sign):
    return [d for d in range(19) if VEL[d][comp] == sign]


XD = (dirs_of(0, 1), dirs_of(0, -1))
YD = (dirs_of(1, 1), dirs_of(1, -1))
ZD = (dirs_of(2, 1), dirs_of(2, -1))
XZD = tuple([d for d in XD[s] if VEL[d][2] != 0] for s in range(2))


def split3(v):
    hi = v.astype(BF16).astype(F32)
    rest = v - hi
    mid = rest.astype(BF16).astype(F32)
    return hi, mid, rest - mid


def dot(a, b, ca, cb):
    return lax.dot_general(a, b, (((ca,), (cb,)), ((), ())), preferred_element_type=F32)


def stacked(v):
    return jnp.concatenate(split3(v), 0).astype(BF16)


def unstacked(v):
    k = v.shape[0] // 3
    return v[0:k] + v[k : 2 * k] + v[2 * k : 3 * k]


def kernel(
    sizes,
    pop_h, *rest,
):
    small_h, (nxt, bnext, pop), rest = rest[:11], rest[11:14], rest[14:]
    small, rest = rest[:11], rest[11:]
    step(sizes, pop_h, small_h, pop, *small, nxt, bnext, *rest)


def step(
    sizes, pop_h, small_h,
    pop, lcell, ldir, lslot, larm, bb_ref, bpos, bquat, bvel, bspin, imass, iinert,
    nxt, bnext,
    relaxed, sendx, xin, sendz, zin, sende, ein, sendy, yin, yflat, ycols,
    dmap, wmap, motion_own, motion_all, tiles, force_all, half, half_in,
    hs, hr, ms, mr, fs, fr, cs, cr, ps, ss,
):
    ngx, ngy = sizes
    owners = ngx * ngy
    span_x, span_z, span_y = pop.shape[1:]
    cells = span_x * span_z
    links = lcell.shape[-1]
    body_own = bvel.shape[1]
    slots = bb_ref.shape[-1]
    a, b, e = lax.axis_index("gx"), lax.axis_index("gy"), lax.axis_index("gz")
    me = a * ngy + b
    ap, am = lax.rem(a + 1, ngx), lax.rem(a + ngx - 1, ngx)
    bp, bm = lax.rem(b + 1, ngy), lax.rem(b + ngy - 1, ngy)
    oe = 1 - e

    def dev(x, y, z):
        return {"gx": x, "gy": y, "gz": z}

    def peer_of(offset):
        p = lax.rem(me + offset, owners)
        return p, dev(p // ngy, lax.rem(p, ngy), e)

    unroll = owners <= 16

    def loop(lo, hi, body):
        if unroll:
            for i in range(lo, hi):
                body(i)
        else:
            pl.loop(lo, hi)(body)

    small = (lcell, ldir, lslot, larm, bb_ref, bpos, bquat, bvel, bspin, imass, iinert)
    small_in = [
        pltpu.make_async_copy(src, dst, ss.at[k]) for k, (src, dst) in enumerate(zip(small_h, small))
    ]
    chunk = span_x // POP_CHUNKS
    pop_in = [
        pltpu.make_async_copy(
            pop_h.at[:, pl.ds(k * chunk, chunk)], pop.at[:, pl.ds(k * chunk, chunk)], ps.at[k]
        )
        for k in range(POP_CHUNKS)
    ]
    for k in (7, 8):
        small_in[k].start()
    for c in pop_in:
        c.start()
    for k in (0, 1, 2, 3, 4, 5, 6, 9, 10):
        small_in[k].start()

    barrier = pltpu.get_barrier_semaphore()

    def greet(o):
        pl.semaphore_signal(barrier, inc=1, device_id=peer_of(o)[1], device_id_type=pl.DeviceIdType.MESH)

    loop(1, owners, greet)
    others = [dev(a, b, oe), dev(ap, b, oe), dev(am, b, oe), dev(a, bp, oe), dev(a, bm, oe)]
    for t in others:
        pl.semaphore_signal(barrier, inc=1, device_id=t, device_id_type=pl.DeviceIdType.MESH)

    small_in[7].wait()
    small_in[8].wait()
    motion_own[...] = jnp.concatenate(
        [bvel[...], bspin[...], jnp.zeros((2, body_own), F32)], 0
    )
    motion_all[me] = motion_own[...]

    for x in range(span_x):
        if x % chunk == 0:
            pop_in[x // chunk].wait()
        for z in range(0, span_z, 8):
            f = [pop[d, x, z : z + 8, :] for d in range(19)]
            rho = f[0]
            for d in range(1, 19):
                rho = rho + f[d]
            inv = 1.0 / rho
            u = []
            for c in range(3):
                pos, neg = dirs_of(c, 1), dirs_of(c, -1)
                tot = f[pos[0]] - f[neg[0]]
                for p, q in zip(pos[1:], neg[1:]):
                    tot = tot + (f[p] - f[q])
                u.append(tot * inv)
            usq = 1.0 - 1.5 * (u[0] * u[0] + u[1] * u[1] + u[2] * u[2])
            rows = pl.ds(x * span_z + z, 8)
            keep = 1.0 - OMEGA
            relaxed[0, rows, :] = keep * f[0] + (OMEGA * WT[0]) * rho * usq
            for d in range(1, 19, 2):
                terms = [u[c] if VEL[d][c] > 0 else -u[c] for c in range(3) if VEL[d][c]]
                proj = terms[0] if len(terms) == 1 else terms[0] + terms[1]
                scale = (OMEGA * WT[d]) * rho
                even = scale * (usq + 4.5 * proj * proj)
                odd = scale * (3.0 * proj)
                relaxed[d, rows, :] = keep * f[d] + (even + odd)
                relaxed[d + 1, rows, :] = keep * f[d + 1] + (even - odd)

    for s in range(2):
        xe = (span_x - 1) if s == 0 else 0
        ze = (span_z - 1) if s == 0 else 0
        for j, d in enumerate(XD[s]):
            sendx[s, j] = relaxed[d, xe * span_z : (xe + 1) * span_z, :]
        for j, d in enumerate(ZD[s]):
            for x in range(span_x):
                r = x * span_z + ze
                sendz[s, j, x : x + 1, :] = relaxed[d, r : r + 1, :]
        sende[s] = jnp.zeros(sende.shape[1:], F32)
        for j, d in enumerate(XZD[s]):
            r = xe * span_z + ((span_z - 1) if VEL[d][2] > 0 else 0)
            sende[s, j : j + 1, :] = relaxed[d, r : r + 1, :]
    lane = lax.broadcasted_iota(jnp.int32, (cells, span_y), 1)
    pack = jnp.zeros((cells, span_y), F32)
    for s in range(2):
        ye = (span_y - 1) if s == 0 else 0
        for j, d in enumerate(YD[s]):
            pack = jnp.where(lane == 8 * s + j, relaxed[d, :, ye : ye + 1], pack)
    pack_t = pack.T
    for s in range(2):
        sendy[s] = pack_t[8 * s : 8 * s + 8, :]

    pl.semaphore_wait(barrier, owners - 1 + len(others))

    def motion_copy(o, slot):
        return pltpu.make_async_remote_copy(
            src_ref=motion_own, dst_ref=motion_all.at[slot], send_sem=ms.at[o], recv_sem=mr.at[slot],
            device_id=peer_of(o)[1], device_id_type=pl.DeviceIdType.MESH,
        )

    loop(1, owners, lambda o: motion_copy(o, me).start())

    halo = []

    def rim(src, dst, target):
        k = len(halo)
        c = pltpu.make_async_remote_copy(
            src_ref=src, dst_ref=dst, send_sem=hs.at[k], recv_sem=hr.at[k],
            device_id=target, device_id_type=pl.DeviceIdType.MESH,
        )
        c.start()
        halo.append(c)

    for s in range(2):
        xt, yt = (ap, bp) if s == 0 else (am, bm)
        rim(sendx.at[s], xin.at[s], dev(xt, b, e))
        rim(sende.at[s], ein.at[s], dev(xt, b, oe))
        rim(sendy.at[s], yin.at[s, 0], dev(a, yt, e))
        rim(sendy.at[s], yin.at[s, 1], dev(ap, yt, e))
        rim(sendy.at[s], yin.at[s, 2], dev(am, yt, e))
        rim(sendy.at[s], yin.at[s, 3], dev(a, yt, oe))
    rim(sendz, zin, dev(a, b, oe))

    for k in (0, 1, 2, 3, 4, 5, 6, 9, 10):
        small_in[k].wait()

    cell = lcell[0, 0]
    dirs = ldir[0, 0]
    row_of = cell // span_y
    lane_of = cell - row_of * span_y
    dirs_f = dirs.astype(F32)
    iota_c = lax.broadcasted_iota(jnp.int32, (cells, links), 0)
    iota_y = lax.broadcasted_iota(jnp.int32, (span_y, links), 0)
    row_t = jnp.where(iota_c == row_of, 1.0, 0.0).astype(BF16)
    lane_mask = iota_y == lane_of
    dmap[...] = dot(row_t, jnp.where(lane_mask, dirs_f, 0.0).astype(BF16), 1, 1)
    dm = dmap[...]
    post_map = jnp.zeros((cells, span_y), F32)
    for d in range(1, 19):
        post_map = jnp.where(dm == float(d), relaxed[d], post_map)
    picked = None
    for part in split3(post_map):
        t = dot(part.astype(BF16), row_t, 0, 0)
        picked = t if picked is None else picked + t
    post = jnp.sum(jnp.where(lane_mask, picked, 0.0), axis=0, keepdims=True)
    iota_s = lax.broadcasted_iota(jnp.int32, (slots, links), 0)
    slot_t = jnp.where(iota_s == lslot[0, 0], 1.0, 0.0).astype(BF16)

    vel = []
    for c in range(3):
        v = jnp.zeros((1, links), F32)
        for d in range(1, 19):
            if VEL[d][c]:
                v = jnp.where(dirs == d, float(VEL[d][c]), v)
        vel.append(v)
    six_w = jnp.where(dirs > 6, 6.0 * WT[7], 6.0 * WT[1])

    def motion_wait(o):
        p, _ = peer_of(o)
        motion_copy(o, p).wait_recv()

    loop(1, owners, motion_wait)
    bodies = bb_ref[0, 0]
    iota_b = lax.broadcasted_iota(jnp.int32, (body_own, slots), 0)

    def owner_onehot(o):
        return jnp.where(iota_b == bodies - o * body_own, 1.0, 0.0).astype(BF16)

    def gather(o, acc):
        return acc + dot(stacked(motion_all[o]), owner_onehot(o), 1, 0)

    slot_motion = unstacked(
        lax.fori_loop(0, owners, gather, jnp.zeros((24, slots), F32), unroll=unroll)
    )
    m = unstacked(dot(stacked(slot_motion), slot_t, 1, 0))
    mv = [m[i : i + 1, :] for i in range(6)]
    arm = [larm[i, 0, 0] for i in range(3)]
    wall = [
        mv[0] + mv[4] * arm[2] - mv[5] * arm[1],
        mv[1] + mv[5] * arm[0] - mv[3] * arm[2],
        mv[2] + mv[3] * arm[1] - mv[4] * arm[0],
    ]
    drop = six_w * (vel[0] * wall[0] + vel[1] * wall[1] + vel[2] * wall[2])
    bounce = post - drop
    live = jnp.where(dirs > 0, 1.0, 0.0)
    exchanged = (post + bounce) * live
    force = [vel[c] * exchanged for c in range(3)]
    torque = [
        arm[1] * force[2] - arm[2] * force[1],
        arm[2] * force[0] - arm[0] * force[2],
        arm[0] * force[1] - arm[1] * force[0],
    ]
    loads = jnp.concatenate(force + torque + [jnp.zeros((2, links), F32)], 0)
    slot_load = unstacked(dot(stacked(loads), slot_t, 1, 1))
    slot_parts = stacked(slot_load)

    def spread(o):
        tiles[o] = unstacked(dot(slot_parts, owner_onehot(o), 1, 1))

    loop(0, owners, spread)

    def force_copy(o, src, slot):
        return pltpu.make_async_remote_copy(
            src_ref=tiles.at[src], dst_ref=force_all.at[slot], send_sem=fs.at[o], recv_sem=fr.at[slot],
            device_id=peer_of(o)[1], device_id_type=pl.DeviceIdType.MESH,
        )

    loop(1, owners, lambda o: force_copy(o, peer_of(o)[0], me).start())
    force_all[me] = tiles[me]

    wm = None
    for part in split3(drop):
        t = dot(row_t, jnp.where(lane_mask, part, 0.0).astype(BF16), 1, 1)
        wm = t if wm is None else wm + t
    wmap[...] = wm

    for c in halo:
        c.wait_recv()
    lane_c = lax.broadcasted_iota(jnp.int32, (8, cells), 1)
    z_c = lane_c - (lane_c // span_z) * span_z
    sub_c = lax.broadcasted_iota(jnp.int32, (8, cells), 0)
    both = []
    for s in range(2):
        t0, t1, t2, t3 = (yin[s, k] for k in range(4))
        out = t0
        for j, d in enumerate(YD[s]):
            cx, _, cz = VEL[d]
            if cx == 1:
                v = jnp.where(lane_c < span_z, pltpu.roll(t1, span_z, 1), pltpu.roll(t0, span_z, 1))
            elif cx == -1:
                v = jnp.where(
                    lane_c >= cells - span_z,
                    pltpu.roll(t2, cells - span_z, 1),
                    pltpu.roll(t0, cells - span_z, 1),
                )
            elif cz == 1:
                v = jnp.where(z_c == 0, pltpu.roll(t3, cells - span_z + 1, 1), pltpu.roll(t0, 1, 1))
            elif cz == -1:
                v = jnp.where(
                    z_c == span_z - 1, pltpu.roll(t3, span_z - 1, 1), pltpu.roll(t0, cells - 1, 1)
                )
            else:
                continue
            out = jnp.where(sub_c == j, v, out)
        both.append(out)
    both.append(jnp.zeros((span_y - 16, cells), F32))
    ycols[...] = jnp.concatenate(both, 0).T

    iz = lax.broadcasted_iota(jnp.int32, (span_z, span_y), 0)
    iy = lax.broadcasted_iota(jnp.int32, (span_z, span_y), 1)
    for x in range(span_x):
        rows = slice(x * span_z, (x + 1) * span_z)
        dm_x = dmap[rows, :]
        wm_x = wmap[rows, :]
        for i in range(19):
            cx, cy, cz = VEL[i]
            sx = x - cx
            inside = 0 <= sx < span_x
            if inside:
                v = relaxed[i, sx * span_z : (sx + 1) * span_z, :]
            else:
                s = 0 if cx > 0 else 1
                v = xin[s, XD[s].index(i)]
            if cz:
                s = 0 if cz > 0 else 1
                if inside:
                    edge = zin[s, ZD[s].index(i), sx : sx + 1, :]
                else:
                    sxx = 0 if cx > 0 else 1
                    j = XZD[sxx].index(i)
                    edge = ein[sxx, j : j + 1, :]
                v = pltpu.roll(v, 1 if cz > 0 else span_z - 1, 0)
                v = jnp.where(iz == (0 if cz > 0 else span_z - 1), edge, v)
            if cy:
                s = 0 if cy > 0 else 1
                j = 8 * s + YD[s].index(i)
                v = pltpu.roll(v, 1 if cy > 0 else span_y - 1, 1)
                v = jnp.where(iy == (0 if cy > 0 else span_y - 1), ycols[rows, j : j + 1], v)
            if i:
                d = OPP[i]
                v = jnp.where(dm_x == float(d), relaxed[d, rows, :] - wm_x, v)
            nxt[i, x] = v

    def force_wait(o):
        p, _ = peer_of(o)
        force_copy(o, p, p).wait_recv()

    loop(1, owners, force_wait)
    half[...] = lax.fori_loop(
        0, owners, lambda o, acc: acc + force_all[o], jnp.zeros(half.shape, F32), unroll=unroll
    )
    swap = pltpu.make_async_remote_copy(
        src_ref=half, dst_ref=half_in, send_sem=cs, recv_sem=cr,
        device_id=dev(a, b, oe), device_id_type=pl.DeviceIdType.MESH,
    )
    swap.start()

    def sent(o):
        motion_copy(o, me).wait_send()
        force_copy(o, peer_of(o)[0], me).wait_send()

    loop(1, owners, sent)
    for c in halo:
        c.wait_send()
    swap.wait()
    load = half[...] + half_in[...]
    f = [load[i : i + 1, :] for i in range(6)]
    pos = [bpos[i : i + 1, :] for i in range(3)]
    qw, qx, qy, qz = (bquat[i : i + 1, :] for i in range(4))
    velo = [bvel[i : i + 1, :] + imass[...] * f[i] for i in range(3)]
    velo[2] = velo[2] - GRAV
    rot = [
        [1.0 - 2.0 * (qy * qy + qz * qz), 2.0 * (qx * qy - qw * qz), 2.0 * (qx * qz + qw * qy)],
        [2.0 * (qx * qy + qw * qz), 1.0 - 2.0 * (qx * qx + qz * qz), 2.0 * (qy * qz - qw * qx)],
        [2.0 * (qx * qz - qw * qy), 2.0 * (qy * qz + qw * qx), 1.0 - 2.0 * (qx * qx + qy * qy)],
    ]
    tq = f[3:6]
    acc = [
        iinert[c : c + 1, :] * (rot[0][c] * tq[0] + rot[1][c] * tq[1] + rot[2][c] * tq[2])
        for c in range(3)
    ]
    spin = [
        bspin[r : r + 1, :] + (rot[r][0] * acc[0] + rot[r][1] * acc[1] + rot[r][2] * acc[2])
        for r in range(3)
    ]
    sx, sy, sz = spin
    dq = [
        -(sx * qx + sy * qy + sz * qz),
        sx * qw + sy * qz - sz * qy,
        sy * qw + sz * qx - sx * qz,
        sz * qw + sx * qy - sy * qx,
    ]
    scale = lax.rsqrt(1.0 + 0.25 * (sx * sx + sy * sy + sz * sz))
    quat = [(q + 0.5 * k) * scale for q, k in zip((qw, qx, qy, qz), dq)]
    result = [pos[i] + velo[i] for i in range(3)] + quat + velo + spin
    for i, v in enumerate(result):
        bnext[i : i + 1, :] = v


def write_out(a, b, a_out, b_out, sems):
    copies = [pltpu.make_async_copy(a, a_out, sems.at[0]), pltpu.make_async_copy(b, b_out, sems.at[1])]
    for c in copies:
        c.start()
    for c in copies:
        c.wait()


def shards(sizes, *args):
    pop = args[0]
    span_x, span_z, span_y = pop.shape[1:]
    cells = span_x * span_z
    body_own = args[6].shape[1]
    owners = sizes[0] * sizes[1]
    args = list(args)
    args[10] = args[10].reshape(1, -1)
    vm = pl.BlockSpec(memory_space=pltpu.VMEM)
    dma = pltpu.SemaphoreType.DMA
    V = lambda *s: pltpu.VMEM(s, F32)
    args = [pltpu.with_memory_space_constraint(v, pltpu.MemorySpace.HBM) for v in args]
    hbm = pl.BlockSpec(memory_space=pltpu.MemorySpace.HBM)
    outs = pl.pallas_call(
        functools.partial(kernel, sizes),
        out_shape=(
            jax.ShapeDtypeStruct(pop.shape, F32),
            jax.ShapeDtypeStruct((13, body_own), F32),
        ),
        in_specs=[hbm] * len(args),
        out_specs=(vm, vm),
        scratch_shapes=[
            *[pltpu.VMEM(v.shape, v.dtype) for v in args],
            V(19, cells, span_y),
            V(2, 5, span_z, span_y), V(2, 5, span_z, span_y),
            V(2, 5, span_x, span_y), V(2, 5, span_x, span_y),
            V(2, 8, span_y), V(2, 8, span_y),
            V(2, 8, cells), V(2, 4, 8, cells),
            V(16, cells), V(cells, span_y),
            V(cells, span_y), V(cells, span_y),
            V(8, body_own), V(owners, 8, body_own),
            V(owners, 8, body_own), V(owners, 8, body_own),
            V(8, body_own), V(8, body_own),
            dma((13,)), dma((13,)),
            dma((owners,)), dma((owners,)),
            dma((owners,)), dma((owners,)),
            dma, dma,
            dma((POP_CHUNKS,)), dma((11,)),
        ],
        compiler_params=pltpu.CompilerParams(
            collective_id=0, has_side_effects=True, vmem_limit_bytes=K1_VMEM
        ),
        name="lattice_step",
    )(*args)
    return pl.pallas_call(
        write_out,
        out_shape=tuple(jax.ShapeDtypeStruct(v.shape, F32) for v in outs),
        in_specs=[vm, vm],
        out_specs=(hbm, hbm),
        scratch_shapes=[dma((2,))],
        compiler_params=pltpu.CompilerParams(vmem_limit_bytes=K2_VMEM),
        name="write_out",
    )(*outs)


def solution(mesh):
    sizes = (mesh.shape["gx"], mesh.shape["gy"])
    link = P("gx", "gz", "gy", None)
    body = P(None, ("gx", "gy"))
    return jax.shard_map(
        functools.partial(shards, sizes),
        mesh=mesh,
        in_specs=(
            P(None, "gx", "gz", "gy"), link, link, link, P(None, "gx", "gz", "gy", None), link,
            body, body, body, body, P(("gx", "gy")), body,
        ),
        out_specs=(P(None, "gx", "gz", "gy"), body),
        check_vma=False,
    )
```

```python
import functools

import jax
import jax.numpy as jnp
import numpy as np
from jax import lax
from jax.experimental import pallas as pl
from jax.experimental.pallas import tpu as pltpu
from jax.sharding import PartitionSpec as P

VEL = [
    (0, 0, 0), (1, 0, 0), (-1, 0, 0), (0, 1, 0), (0, -1, 0), (0, 0, 1), (0, 0, -1),
    (1, 1, 0), (-1, -1, 0), (1, -1, 0), (-1, 1, 0), (1, 0, 1), (-1, 0, -1), (1, 0, -1),
    (-1, 0, 1), (0, 1, 1), (0, -1, -1), (0, 1, -1), (0, -1, 1),
]
WT = [1.0 / 3.0] + [1.0 / 18.0] * 6 + [1.0 / 36.0] * 12
OPP = [0, 2, 1, 4, 3, 6, 5, 8, 7, 10, 9, 12, 11, 14, 13, 16, 15, 18, 17]
OMEGA = 1.25
POP_CHUNKS = 2
K1_VMEM = 48 * 1024 * 1024
K2_VMEM = 1024 * 1024
GRAV = 0.02
F32 = jnp.float32
BF16 = jnp.bfloat16


def dirs_of(comp, sign):
    return [d for d in range(19) if VEL[d][comp] == sign]


XD = (dirs_of(0, 1), dirs_of(0, -1))
YD = (dirs_of(1, 1), dirs_of(1, -1))
ZD = (dirs_of(2, 1), dirs_of(2, -1))
XZD = tuple([d for d in XD[s] if VEL[d][2] != 0] for s in range(2))


def split3(v):
    hi = v.astype(BF16).astype(F32)
    rest = v - hi
    mid = rest.astype(BF16).astype(F32)
    return hi, mid, rest - mid


def dot(a, b, ca, cb):
    return lax.dot_general(a, b, (((ca,), (cb,)), ((), ())), preferred_element_type=F32)


def stacked(v):
    return jnp.concatenate(split3(v), 0).astype(BF16)


def unstacked(v):
    k = v.shape[0] // 3
    return v[0:k] + v[k : 2 * k] + v[2 * k : 3 * k]


def kernel(
    sizes,
    pop_h, *rest,
):
    small_h, (nxt, bnext, pop), rest = rest[:11], rest[11:14], rest[14:]
    small, rest = rest[:11], rest[11:]
    step(sizes, pop_h, small_h, pop, *small, nxt, bnext, *rest)


def step(
    sizes, pop_h, small_h,
    pop, lcell, ldir, lslot, larm, bb_ref, bpos, bquat, bvel, bspin, imass, iinert,
    nxt, bnext,
    relaxed, sendx, xin, sendz, zin, sende, ein, sendy, yin, yflat, ycols,
    dmap, wmap, motion_own, motion_all, tiles, plane_in, plane_sum, line_in,
    hs, hr, ms, mr, fs, fr, cs, cr, ps, ss,
):
    ngx, ngy, ngz = sizes
    hb = ngy // ngz
    owners = ngx * ngy
    span_x, span_z, span_y = pop.shape[1:]
    cells = span_x * span_z
    links = lcell.shape[-1]
    body_own = bvel.shape[1]
    slots = bb_ref.shape[-1]
    a, b, e = lax.axis_index("gx"), lax.axis_index("gy"), lax.axis_index("gz")
    me = a * ngy + b
    ap, am = lax.rem(a + 1, ngx), lax.rem(a + ngx - 1, ngx)
    bp, bm = lax.rem(b + 1, ngy), lax.rem(b + ngy - 1, ngy)
    oe = 1 - e

    def dev(x, y, z):
        return {"gx": x, "gy": y, "gz": z}

    def step_of(index, count, k):
        if count & (count - 1) == 0:
            return jnp.bitwise_xor(index, k)
        return lax.rem(index + k, count)

    plane = [(k, z) for k in range(ngx) for z in range(ngz) if k or z]
    line = list(range(1, ngy))

    def plane_dev(k, z):
        return step_of(a, ngx, k), step_of(e, ngz, z)

    unroll = owners <= 16

    def loop(lo, hi, body):
        if unroll:
            for i in range(lo, hi):
                body(i)
        else:
            pl.loop(lo, hi)(body)

    barrier = pltpu.get_barrier_semaphore()
    greeted = [dev(a, step_of(b, ngy, k), z) for k in reversed(line) for z in range(ngz)]
    for k, z in reversed(plane):
        x, w = plane_dev(k, z)
        greeted.append(dev(x, b, w))
    for t in greeted:
        pl.semaphore_signal(barrier, inc=1, device_id=t, device_id_type=pl.DeviceIdType.MESH)

    small = (lcell, ldir, lslot, larm, bb_ref, bpos, bquat, bvel, bspin, imass, iinert)
    small_in = [
        pltpu.make_async_copy(src, dst, ss.at[k]) for k, (src, dst) in enumerate(zip(small_h, small))
    ]
    chunk = span_x // POP_CHUNKS
    pop_in = [
        pltpu.make_async_copy(
            pop_h.at[:, pl.ds(k * chunk, chunk)], pop.at[:, pl.ds(k * chunk, chunk)], ps.at[k]
        )
        for k in range(POP_CHUNKS)
    ]
    for k in (7, 8):
        small_in[k].start()
    for c in pop_in:
        c.start()
    for k in (0, 1, 2, 3, 4, 5, 6, 9, 10):
        small_in[k].start()

    small_in[7].wait()
    small_in[8].wait()
    motion_own[...] = jnp.concatenate(
        [bvel[...], bspin[...], jnp.zeros((2, body_own), F32)], 0
    )
    motion_all[me] = motion_own[...]

    for x in range(span_x):
        if x % chunk == 0:
            pop_in[x // chunk].wait()
        for z in range(0, span_z, 8):
            f = [pop[d, x, z : z + 8, :] for d in range(19)]
            rho = f[0]
            for d in range(1, 19):
                rho = rho + f[d]
            inv = 1.0 / rho
            u = []
            for c in range(3):
                pos, neg = dirs_of(c, 1), dirs_of(c, -1)
                tot = f[pos[0]] - f[neg[0]]
                for p, q in zip(pos[1:], neg[1:]):
                    tot = tot + (f[p] - f[q])
                u.append(tot * inv)
            usq = 1.0 - 1.5 * (u[0] * u[0] + u[1] * u[1] + u[2] * u[2])
            rows = pl.ds(x * span_z + z, 8)
            keep = 1.0 - OMEGA
            relaxed[0, rows, :] = keep * f[0] + (OMEGA * WT[0]) * rho * usq
            for d in range(1, 19, 2):
                terms = [u[c] if VEL[d][c] > 0 else -u[c] for c in range(3) if VEL[d][c]]
                proj = terms[0] if len(terms) == 1 else terms[0] + terms[1]
                scale = (OMEGA * WT[d]) * rho
                even = scale * (usq + 4.5 * proj * proj)
                odd = scale * (3.0 * proj)
                relaxed[d, rows, :] = keep * f[d] + (even + odd)
                relaxed[d + 1, rows, :] = keep * f[d + 1] + (even - odd)

    for s in range(2):
        xe = (span_x - 1) if s == 0 else 0
        ze = (span_z - 1) if s == 0 else 0
        for j, d in enumerate(XD[s]):
            sendx[s, j] = relaxed[d, xe * span_z : (xe + 1) * span_z, :]
        for j, d in enumerate(ZD[s]):
            for x in range(span_x):
                r = x * span_z + ze
                sendz[s, j, x : x + 1, :] = relaxed[d, r : r + 1, :]
        sende[s] = jnp.zeros(sende.shape[1:], F32)
        for j, d in enumerate(XZD[s]):
            r = xe * span_z + ((span_z - 1) if VEL[d][2] > 0 else 0)
            sende[s, j : j + 1, :] = relaxed[d, r : r + 1, :]
    lane = lax.broadcasted_iota(jnp.int32, (cells, span_y), 1)
    pack = jnp.zeros((cells, span_y), F32)
    for s in range(2):
        ye = (span_y - 1) if s == 0 else 0
        for j, d in enumerate(YD[s]):
            pack = jnp.where(lane == 8 * s + j, relaxed[d, :, ye : ye + 1], pack)
    pack_t = pack.T
    for s in range(2):
        sendy[s] = pack_t[8 * s : 8 * s + 8, :]

    pl.semaphore_wait(barrier, len(greeted))

    def motion_line(k, slot):
        return pltpu.make_async_remote_copy(
            src_ref=motion_own, dst_ref=motion_all.at[slot], send_sem=ms.at[k], recv_sem=mr.at[slot],
            device_id=dev(a, step_of(b, ngy, k), e), device_id_type=pl.DeviceIdType.MESH,
        )

    def motion_plane(k, kb, src, slot):
        return pltpu.make_async_remote_copy(
            src_ref=src, dst_ref=motion_all.at[slot],
            send_sem=ms.at[k * ngy + kb], recv_sem=mr.at[slot],
            device_id=dev(step_of(a, ngx, k), b, e), device_id_type=pl.DeviceIdType.MESH,
        )

    for k in reversed(line):
        motion_line(k, me).start()
    for k in range(1, ngx):
        motion_plane(k, 0, motion_own, me).start()

    halo = []

    def rim(src, dst, target):
        k = len(halo)
        c = pltpu.make_async_remote_copy(
            src_ref=src, dst_ref=dst, send_sem=hs.at[k], recv_sem=hr.at[k],
            device_id=target, device_id_type=pl.DeviceIdType.MESH,
        )
        c.start()
        halo.append(c)
        return c

    y_rims = []

    for s in range(2):
        xt, yt = (ap, bp) if s == 0 else (am, bm)
        rim(sendx.at[s], xin.at[s], dev(xt, b, e))
        rim(sende.at[s], ein.at[s], dev(xt, b, oe))
        y_rims.append(rim(sendy.at[s], yin.at[s, 0], dev(a, yt, e)))
    rim(sendz, zin, dev(a, b, oe))

    for k in (0, 1, 2, 3, 4, 5, 6, 9, 10):
        small_in[k].wait()

    cell = lcell[0, 0]
    dirs = ldir[0, 0]
    row_of = cell // span_y
    lane_of = cell - row_of * span_y
    dirs_f = dirs.astype(F32)
    iota_c = lax.broadcasted_iota(jnp.int32, (cells, links), 0)
    iota_y = lax.broadcasted_iota(jnp.int32, (span_y, links), 0)
    row_t = jnp.where(iota_c == row_of, 1.0, 0.0).astype(BF16)
    lane_mask = iota_y == lane_of
    dmap[...] = dot(row_t, jnp.where(lane_mask, dirs_f, 0.0).astype(BF16), 1, 1)
    dm = dmap[...]
    post_map = jnp.zeros((cells, span_y), F32)
    for d in range(1, 19):
        post_map = jnp.where(dm == float(d), relaxed[d], post_map)
    picked = None
    for part in split3(post_map):
        t = dot(part.astype(BF16), row_t, 0, 0)
        picked = t if picked is None else picked + t
    post = jnp.sum(jnp.where(lane_mask, picked, 0.0), axis=0, keepdims=True)
    iota_s = lax.broadcasted_iota(jnp.int32, (slots, links), 0)
    slot_t = jnp.where(iota_s == lslot[0, 0], 1.0, 0.0).astype(BF16)

    for kb in line:
        slot = a * ngy + step_of(b, ngy, kb)
        motion_line(kb, slot).wait_recv()
        for k in range(1, ngx):
            motion_plane(k, kb, motion_all.at[slot], slot).start()
    first = [c for c in halo if all(c is not r for r in y_rims)]
    for c in y_rims:
        c.wait_recv()
    for s in range(2):
        rim(yin.at[s, 0], yin.at[s, 1], dev(ap, b, e))
        rim(yin.at[s, 0], yin.at[s, 2], dev(am, b, e))
        rim(yin.at[s, 0], yin.at[s, 3], dev(a, b, oe))
    second = halo[len(first) + len(y_rims) :]

    vel = []
    for c in range(3):
        v = jnp.zeros((1, links), F32)
        for d in range(1, 19):
            if VEL[d][c]:
                v = jnp.where(dirs == d, float(VEL[d][c]), v)
        vel.append(v)
    six_w = jnp.where(dirs > 6, 6.0 * WT[7], 6.0 * WT[1])

    for kb in range(ngy):
        for k in range(1, ngx):
            slot = step_of(a, ngx, k) * ngy + step_of(b, ngy, kb)
            motion_plane(k, kb, motion_own, slot).wait_recv()
    bodies = bb_ref[0, 0]
    iota_b = lax.broadcasted_iota(jnp.int32, (body_own, slots), 0)

    def owner_onehot(o):
        return jnp.where(iota_b == bodies - o * body_own, 1.0, 0.0).astype(BF16)

    def gather(o, acc):
        return acc + dot(stacked(motion_all[o]), owner_onehot(o), 1, 0)

    slot_motion = unstacked(
        lax.fori_loop(0, owners, gather, jnp.zeros((24, slots), F32), unroll=unroll)
    )
    m = unstacked(dot(stacked(slot_motion), slot_t, 1, 0))
    mv = [m[i : i + 1, :] for i in range(6)]
    arm = [larm[i, 0, 0] for i in range(3)]
    wall = [
        mv[0] + mv[4] * arm[2] - mv[5] * arm[1],
        mv[1] + mv[5] * arm[0] - mv[3] * arm[2],
        mv[2] + mv[3] * arm[1] - mv[4] * arm[0],
    ]
    drop = six_w * (vel[0] * wall[0] + vel[1] * wall[1] + vel[2] * wall[2])
    bounce = post - drop
    live = jnp.where(dirs > 0, 1.0, 0.0)
    exchanged = (post + bounce) * live
    force = [vel[c] * exchanged for c in range(3)]
    torque = [
        arm[1] * force[2] - arm[2] * force[1],
        arm[2] * force[0] - arm[0] * force[2],
        arm[0] * force[1] - arm[1] * force[0],
    ]
    loads = jnp.concatenate(force + torque + [jnp.zeros((2, links), F32)], 0)
    slot_load = unstacked(dot(stacked(loads), slot_t, 1, 1))
    slot_parts = stacked(slot_load)

    def spread(o):
        tiles[o] = unstacked(dot(slot_parts, owner_onehot(o), 1, 1))

    loop(0, owners, spread)

    here = a * ngz + e

    def force_plane(k, z, slot):
        x, w = plane_dev(k, z)
        return pltpu.make_async_remote_copy(
            src_ref=tiles.at[pl.ds(x * ngy + w * hb, hb)], dst_ref=plane_in.at[slot],
            send_sem=fs.at[k * ngz + z], recv_sem=fr.at[slot],
            device_id=dev(x, b, w), device_id_type=pl.DeviceIdType.MESH,
        )

    for k, z in reversed(plane):
        force_plane(k, z, here).start()
    for k in range(hb):
        plane_in[here, k] = tiles[a * ngy + e * hb + k]

    wm = None
    for part in split3(drop):
        t = dot(row_t, jnp.where(lane_mask, part, 0.0).astype(BF16), 1, 1)
        wm = t if wm is None else wm + t
    wmap[...] = wm

    for c in first + second:
        c.wait_recv()
    lane_c = lax.broadcasted_iota(jnp.int32, (8, cells), 1)
    z_c = lane_c - (lane_c // span_z) * span_z
    sub_c = lax.broadcasted_iota(jnp.int32, (8, cells), 0)
    both = []
    for s in range(2):
        t0, t1, t2, t3 = (yin[s, k] for k in range(4))
        out = t0
        for j, d in enumerate(YD[s]):
            cx, _, cz = VEL[d]
            if cx == 1:
                v = jnp.where(lane_c < span_z, pltpu.roll(t1, span_z, 1), pltpu.roll(t0, span_z, 1))
            elif cx == -1:
                v = jnp.where(
                    lane_c >= cells - span_z,
                    pltpu.roll(t2, cells - span_z, 1),
                    pltpu.roll(t0, cells - span_z, 1),
                )
            elif cz == 1:
                v = jnp.where(z_c == 0, pltpu.roll(t3, cells - span_z + 1, 1), pltpu.roll(t0, 1, 1))
            elif cz == -1:
                v = jnp.where(
                    z_c == span_z - 1, pltpu.roll(t3, span_z - 1, 1), pltpu.roll(t0, cells - 1, 1)
                )
            else:
                continue
            out = jnp.where(sub_c == j, v, out)
        both.append(out)
    both.append(jnp.zeros((span_y - 16, cells), F32))
    ycols[...] = jnp.concatenate(both, 0).T

    iz = lax.broadcasted_iota(jnp.int32, (span_z, span_y), 0)
    iy = lax.broadcasted_iota(jnp.int32, (span_z, span_y), 1)

    def stream(x):
        rows = slice(x * span_z, (x + 1) * span_z)
        dm_x = dmap[rows, :]
        wm_x = wmap[rows, :]
        for i in range(19):
            cx, cy, cz = VEL[i]
            sx = x - cx
            inside = 0 <= sx < span_x
            if inside:
                v = relaxed[i, sx * span_z : (sx + 1) * span_z, :]
            else:
                s = 0 if cx > 0 else 1
                v = xin[s, XD[s].index(i)]
            if cz:
                s = 0 if cz > 0 else 1
                if inside:
                    edge = zin[s, ZD[s].index(i), sx : sx + 1, :]
                else:
                    sxx = 0 if cx > 0 else 1
                    j = XZD[sxx].index(i)
                    edge = ein[sxx, j : j + 1, :]
                v = pltpu.roll(v, 1 if cz > 0 else span_z - 1, 0)
                v = jnp.where(iz == (0 if cz > 0 else span_z - 1), edge, v)
            if cy:
                s = 0 if cy > 0 else 1
                j = 8 * s + YD[s].index(i)
                v = pltpu.roll(v, 1 if cy > 0 else span_y - 1, 1)
                v = jnp.where(iy == (0 if cy > 0 else span_y - 1), ycols[rows, j : j + 1], v)
            if i:
                d = OPP[i]
                v = jnp.where(dm_x == float(d), relaxed[d, rows, :] - wm_x, v)
            nxt[i, x] = v

    for x in range(span_x // 2):
        stream(x)

    for k, z in plane:
        x, w = plane_dev(k, z)
        force_plane(k, z, x * ngz + w).wait_recv()
    total = plane_in[0]
    for k in range(1, ngx * ngz):
        total = total + plane_in[k]
    plane_sum[...] = total

    def force_line(k, z, src_b):
        return pltpu.make_async_remote_copy(
            src_ref=plane_sum.at[k], dst_ref=line_in.at[src_b],
            send_sem=cs.at[k * ngz + z], recv_sem=cr.at[src_b],
            device_id=dev(a, e * hb + k, z), device_id_type=pl.DeviceIdType.MESH,
        )

    for k in range(hb):
        for z in range(ngz):
            mine = (e * hb + k == b) & (e == z)

            @pl.when(jnp.logical_not(mine))
            def _():
                force_line(k, z, b).start()

            @pl.when(mine)
            def _():
                line_in[b] = plane_sum[k]

    for x in range(span_x // 2, span_x):
        stream(x)

    for k in line:
        motion_line(k, me).wait_send()
    for kb in range(ngy):
        for k in range(1, ngx):
            motion_plane(k, kb, motion_own, me).wait_send()
    for k, z in plane:
        force_plane(k, z, here).wait_send()
    for c in halo:
        c.wait_send()
    for src in range(ngy):
        local = (b // hb == e) & (b == src)

        @pl.when(jnp.logical_not(local))
        def _():
            force_line(0, 0, src).wait_recv()

    load = line_in[0]
    for k in range(1, ngy):
        load = load + line_in[k]
    for k in range(hb):
        for z in range(ngz):
            mine = (e * hb + k == b) & (e == z)

            @pl.when(jnp.logical_not(mine))
            def _():
                force_line(k, z, b).wait_send()

    f = [load[i : i + 1, :] for i in range(6)]
    pos = [bpos[i : i + 1, :] for i in range(3)]
    qw, qx, qy, qz = (bquat[i : i + 1, :] for i in range(4))
    velo = [bvel[i : i + 1, :] + imass[...] * f[i] for i in range(3)]
    velo[2] = velo[2] - GRAV
    rot = [
        [1.0 - 2.0 * (qy * qy + qz * qz), 2.0 * (qx * qy - qw * qz), 2.0 * (qx * qz + qw * qy)],
        [2.0 * (qx * qy + qw * qz), 1.0 - 2.0 * (qx * qx + qz * qz), 2.0 * (qy * qz - qw * qx)],
        [2.0 * (qx * qz - qw * qy), 2.0 * (qy * qz + qw * qx), 1.0 - 2.0 * (qx * qx + qy * qy)],
    ]
    tq = f[3:6]
    acc = [
        iinert[c : c + 1, :] * (rot[0][c] * tq[0] + rot[1][c] * tq[1] + rot[2][c] * tq[2])
        for c in range(3)
    ]
    spin = [
        bspin[r : r + 1, :] + (rot[r][0] * acc[0] + rot[r][1] * acc[1] + rot[r][2] * acc[2])
        for r in range(3)
    ]
    sx, sy, sz = spin
    dq = [
        -(sx * qx + sy * qy + sz * qz),
        sx * qw + sy * qz - sz * qy,
        sy * qw + sz * qx - sx * qz,
        sz * qw + sx * qy - sy * qx,
    ]
    scale = lax.rsqrt(1.0 + 0.25 * (sx * sx + sy * sy + sz * sz))
    quat = [(q + 0.5 * k) * scale for q, k in zip((qw, qx, qy, qz), dq)]
    result = [pos[i] + velo[i] for i in range(3)] + quat + velo + spin
    for i, v in enumerate(result):
        bnext[i : i + 1, :] = v


def write_out(a, b, a_out, b_out, sems):
    copies = [pltpu.make_async_copy(a, a_out, sems.at[0]), pltpu.make_async_copy(b, b_out, sems.at[1])]
    for c in copies:
        c.start()
    for c in copies:
        c.wait()


def shards(sizes, *args):
    pop = args[0]
    span_x, span_z, span_y = pop.shape[1:]
    cells = span_x * span_z
    body_own = args[6].shape[1]
    ngx, ngy, ngz = sizes
    owners = ngx * ngy
    args = list(args)
    args[10] = args[10].reshape(1, -1)
    vm = pl.BlockSpec(memory_space=pltpu.VMEM)
    dma = pltpu.SemaphoreType.DMA
    V = lambda *s: pltpu.VMEM(s, F32)
    args = [pltpu.with_memory_space_constraint(v, pltpu.MemorySpace.HBM) for v in args]
    hbm = pl.BlockSpec(memory_space=pltpu.MemorySpace.HBM)
    outs = pl.pallas_call(
        functools.partial(kernel, sizes),
        out_shape=(
            jax.ShapeDtypeStruct(pop.shape, F32),
            jax.ShapeDtypeStruct((13, body_own), F32),
        ),
        in_specs=[hbm] * len(args),
        out_specs=(vm, vm),
        scratch_shapes=[
            *[pltpu.VMEM(v.shape, v.dtype) for v in args],
            V(19, cells, span_y),
            V(2, 5, span_z, span_y), V(2, 5, span_z, span_y),
            V(2, 5, span_x, span_y), V(2, 5, span_x, span_y),
            V(2, 8, span_y), V(2, 8, span_y),
            V(2, 8, cells), V(2, 4, 8, cells),
            V(16, cells), V(cells, span_y),
            V(cells, span_y), V(cells, span_y),
            V(8, body_own), V(owners, 8, body_own),
            V(owners, 8, body_own), V(ngx * ngz, ngy // ngz, 8, body_own),
            V(ngy // ngz, 8, body_own), V(ngy, 8, body_own),
            dma((13,)), dma((13,)),
            dma((owners,)), dma((owners,)),
            dma((ngx * ngz,)), dma((ngx * ngz,)),
            dma((ngy,)), dma((ngy,)),
            dma((POP_CHUNKS,)), dma((11,)),
        ],
        compiler_params=pltpu.CompilerParams(
            collective_id=0, has_side_effects=True, vmem_limit_bytes=K1_VMEM
        ),
        name="lattice_step",
    )(*args)
    return pl.pallas_call(
        write_out,
        out_shape=tuple(jax.ShapeDtypeStruct(v.shape, F32) for v in outs),
        in_specs=[vm, vm],
        out_specs=(hbm, hbm),
        scratch_shapes=[dma((2,))],
        compiler_params=pltpu.CompilerParams(vmem_limit_bytes=K2_VMEM),
        name="write_out",
    )(*outs)


def solution(mesh):
    sizes = (mesh.shape["gx"], mesh.shape["gy"], mesh.shape["gz"])
    link = P("gx", "gz", "gy", None)
    body = P(None, ("gx", "gy"))
    return jax.shard_map(
        functools.partial(shards, sizes),
        mesh=mesh,
        in_specs=(
            P(None, "gx", "gz", "gy"), link, link, link, P(None, "gx", "gz", "gy", None), link,
            body, body, body, body, P(("gx", "gy")), body,
        ),
        out_specs=(P(None, "gx", "gz", "gy"), body),
        check_vma=False,
    )
```

```python
import functools

import jax
import jax.numpy as jnp
import numpy as np
from jax import lax
from jax.experimental import pallas as pl
from jax.experimental.pallas import tpu as pltpu
from jax.sharding import PartitionSpec as P

VEL = [
    (0, 0, 0), (1, 0, 0), (-1, 0, 0), (0, 1, 0), (0, -1, 0), (0, 0, 1), (0, 0, -1),
    (1, 1, 0), (-1, -1, 0), (1, -1, 0), (-1, 1, 0), (1, 0, 1), (-1, 0, -1), (1, 0, -1),
    (-1, 0, 1), (0, 1, 1), (0, -1, -1), (0, 1, -1), (0, -1, 1),
]
WT = [1.0 / 3.0] + [1.0 / 18.0] * 6 + [1.0 / 36.0] * 12
OPP = [0, 2, 1, 4, 3, 6, 5, 8, 7, 10, 9, 12, 11, 14, 13, 16, 15, 18, 17]
OMEGA = 1.25
POP_CHUNKS = 2
K1_VMEM = 48 * 1024 * 1024
K2_VMEM = 1024 * 1024
GRAV = 0.02
F32 = jnp.float32
BF16 = jnp.bfloat16


def dirs_of(comp, sign):
    return [d for d in range(19) if VEL[d][comp] == sign]


XD = (dirs_of(0, 1), dirs_of(0, -1))
YD = (dirs_of(1, 1), dirs_of(1, -1))
ZD = (dirs_of(2, 1), dirs_of(2, -1))
XZD = tuple([d for d in XD[s] if VEL[d][2] != 0] for s in range(2))


def split3(v):
    hi = v.astype(BF16).astype(F32)
    rest = v - hi
    mid = rest.astype(BF16).astype(F32)
    return hi, mid, rest - mid


def dot(a, b, ca, cb):
    return lax.dot_general(a, b, (((ca,), (cb,)), ((), ())), preferred_element_type=F32)


def stacked(v):
    return jnp.concatenate(split3(v), 0).astype(BF16)


def unstacked(v):
    k = v.shape[0] // 3
    return v[0:k] + v[k : 2 * k] + v[2 * k : 3 * k]


def kernel(
    sizes,
    pop_h, *rest,
):
    small_h, (nxt, bnext, pop), rest = rest[:11], rest[11:14], rest[14:]
    small, rest = rest[:11], rest[11:]
    step(sizes, pop_h, small_h, pop, *small, nxt, bnext, *rest)


def step(
    sizes, pop_h, small_h,
    pop, lcell, ldir, lslot, larm, bb_ref, bpos, bquat, bvel, bspin, imass, iinert,
    nxt, bnext,
    relaxed, sendx, xin, sendz, zin, sende, ein, sendy, yin, yflat, ycols,
    dmap, wmap, motion_own, motion_all, tiles, plane_in, plane_sum, line_in, picks,
    hs, hr, ms, mr, fs, fr, cs, cr, ps, ss,
):
    ngx, ngy, ngz = sizes
    hb = ngy // ngz
    owners = ngx * ngy
    span_x, span_z, span_y = pop.shape[1:]
    cells = span_x * span_z
    links = lcell.shape[-1]
    body_own = bvel.shape[1]
    slots = bb_ref.shape[-1]
    a, b, e = lax.axis_index("gx"), lax.axis_index("gy"), lax.axis_index("gz")
    me = a * ngy + b
    ap, am = lax.rem(a + 1, ngx), lax.rem(a + ngx - 1, ngx)
    bp, bm = lax.rem(b + 1, ngy), lax.rem(b + ngy - 1, ngy)
    oe = 1 - e

    def dev(x, y, z):
        return {"gx": x, "gy": y, "gz": z}

    def peer_of(offset):
        p = lax.rem(me + offset, owners)
        return p, dev(p // ngy, lax.rem(p, ngy), e)

    def step_of(index, count, k):
        if count & (count - 1) == 0:
            return jnp.bitwise_xor(index, k)
        return lax.rem(index + k, count)

    plane = [(k, z) for k in range(ngx) for z in range(ngz) if k or z]
    line = list(range(1, ngy))

    def plane_dev(k, z):
        return step_of(a, ngx, k), step_of(e, ngz, z)

    unroll = owners <= 16

    def loop(lo, hi, body):
        if unroll:
            for i in range(lo, hi):
                body(i)
        else:
            pl.loop(lo, hi)(body)

    barrier = pltpu.get_barrier_semaphore()

    def greet(o):
        pl.semaphore_signal(barrier, inc=1, device_id=peer_of(o)[1], device_id_type=pl.DeviceIdType.MESH)

    loop(1, owners, greet)
    others = [dev(step_of(a, ngx, k), b, oe) for k in range(ngx)]
    others += [dev(a, step_of(b, ngy, k), oe) for k in line]
    for t in others:
        pl.semaphore_signal(barrier, inc=1, device_id=t, device_id_type=pl.DeviceIdType.MESH)

    small = (lcell, ldir, lslot, larm, bb_ref, bpos, bquat, bvel, bspin, imass, iinert)
    small_in = [
        pltpu.make_async_copy(src, dst, ss.at[k]) for k, (src, dst) in enumerate(zip(small_h, small))
    ]
    chunk = span_x // POP_CHUNKS
    pop_in = [
        pltpu.make_async_copy(
            pop_h.at[:, pl.ds(k * chunk, chunk)], pop.at[:, pl.ds(k * chunk, chunk)], ps.at[k]
        )
        for k in range(POP_CHUNKS)
    ]
    for k in (7, 8):
        small_in[k].start()
    for c in pop_in:
        c.start()
    for k in (0, 1, 2, 3, 4, 5, 6, 9, 10):
        small_in[k].start()

    small_in[7].wait()
    small_in[8].wait()
    motion_own[...] = jnp.concatenate(
        [bvel[...], bspin[...], jnp.zeros((2, body_own), F32)], 0
    )
    motion_all[me] = motion_own[...]

    for x in range(span_x):
        if x % chunk == 0:
            pop_in[x // chunk].wait()
        for z in range(0, span_z, 8):
            f = [pop[d, x, z : z + 8, :] for d in range(19)]
            rho = f[0]
            for d in range(1, 19):
                rho = rho + f[d]
            inv = 1.0 / rho
            u = []
            for c in range(3):
                pos, neg = dirs_of(c, 1), dirs_of(c, -1)
                tot = f[pos[0]] - f[neg[0]]
                for p, q in zip(pos[1:], neg[1:]):
                    tot = tot + (f[p] - f[q])
                u.append(tot * inv)
            usq = 1.0 - 1.5 * (u[0] * u[0] + u[1] * u[1] + u[2] * u[2])
            rows = pl.ds(x * span_z + z, 8)
            keep = 1.0 - OMEGA
            relaxed[0, rows, :] = keep * f[0] + (OMEGA * WT[0]) * rho * usq
            for d in range(1, 19, 2):
                terms = [u[c] if VEL[d][c] > 0 else -u[c] for c in range(3) if VEL[d][c]]
                proj = terms[0] if len(terms) == 1 else terms[0] + terms[1]
                scale = (OMEGA * WT[d]) * rho
                even = scale * (usq + 4.5 * proj * proj)
                odd = scale * (3.0 * proj)
                relaxed[d, rows, :] = keep * f[d] + (even + odd)
                relaxed[d + 1, rows, :] = keep * f[d + 1] + (even - odd)

    for s in range(2):
        xe = (span_x - 1) if s == 0 else 0
        ze = (span_z - 1) if s == 0 else 0
        for j, d in enumerate(XD[s]):
            sendx[s, j] = relaxed[d, xe * span_z : (xe + 1) * span_z, :]
        for j, d in enumerate(ZD[s]):
            for x in range(span_x):
                r = x * span_z + ze
                sendz[s, j, x : x + 1, :] = relaxed[d, r : r + 1, :]
        sende[s] = jnp.zeros(sende.shape[1:], F32)
        for j, d in enumerate(XZD[s]):
            r = xe * span_z + ((span_z - 1) if VEL[d][2] > 0 else 0)
            sende[s, j : j + 1, :] = relaxed[d, r : r + 1, :]
    lane = lax.broadcasted_iota(jnp.int32, (cells, span_y), 1)
    pack = jnp.zeros((cells, span_y), F32)
    for s in range(2):
        ye = (span_y - 1) if s == 0 else 0
        for j, d in enumerate(YD[s]):
            pack = jnp.where(lane == 8 * s + j, relaxed[d, :, ye : ye + 1], pack)
    pack_t = pack.T
    for s in range(2):
        sendy[s] = pack_t[8 * s : 8 * s + 8, :]

    pl.semaphore_wait(barrier, owners - 1 + len(others))

    def motion_copy(o, slot):
        return pltpu.make_async_remote_copy(
            src_ref=motion_own, dst_ref=motion_all.at[slot], send_sem=ms.at[o], recv_sem=mr.at[slot],
            device_id=peer_of(o)[1], device_id_type=pl.DeviceIdType.MESH,
        )

    loop(1, owners, lambda o: motion_copy(o, me).start())

    halo = []

    def rim(src, dst, target):
        k = len(halo)
        c = pltpu.make_async_remote_copy(
            src_ref=src, dst_ref=dst, send_sem=hs.at[k], recv_sem=hr.at[k],
            device_id=target, device_id_type=pl.DeviceIdType.MESH,
        )
        c.start()
        halo.append(c)

    for s in range(2):
        xt, yt = (ap, bp) if s == 0 else (am, bm)
        rim(sendx.at[s], xin.at[s], dev(xt, b, e))
        rim(sende.at[s], ein.at[s], dev(xt, b, oe))
        rim(sendy.at[s], yin.at[s, 0], dev(a, yt, e))
        rim(sendy.at[s], yin.at[s, 1], dev(ap, yt, e))
        rim(sendy.at[s], yin.at[s, 2], dev(am, yt, e))
        rim(sendy.at[s], yin.at[s, 3], dev(a, yt, oe))
    rim(sendz, zin, dev(a, b, oe))

    for k in (0, 1, 2, 3, 4, 5, 6, 9, 10):
        small_in[k].wait()

    cell = lcell[0, 0]
    dirs = ldir[0, 0]
    row_of = cell // span_y
    lane_of = cell - row_of * span_y
    dirs_f = dirs.astype(F32)
    iota_c = lax.broadcasted_iota(jnp.int32, (cells, links), 0)
    iota_y = lax.broadcasted_iota(jnp.int32, (span_y, links), 0)
    row_t = jnp.where(iota_c == row_of, 1.0, 0.0).astype(BF16)
    lane_mask = iota_y == lane_of
    dmap[...] = dot(row_t, jnp.where(lane_mask, dirs_f, 0.0).astype(BF16), 1, 1)
    dm = dmap[...]
    post_map = jnp.zeros((cells, span_y), F32)
    for d in range(1, 19):
        post_map = jnp.where(dm == float(d), relaxed[d], post_map)
    picked = None
    for part in split3(post_map):
        t = dot(part.astype(BF16), row_t, 0, 0)
        picked = t if picked is None else picked + t
    post = jnp.sum(jnp.where(lane_mask, picked, 0.0), axis=0, keepdims=True)
    iota_s = lax.broadcasted_iota(jnp.int32, (slots, links), 0)
    slot_t = jnp.where(iota_s == lslot[0, 0], 1.0, 0.0).astype(BF16)

    vel = []
    for c in range(3):
        v = jnp.zeros((1, links), F32)
        for d in range(1, 19):
            if VEL[d][c]:
                v = jnp.where(dirs == d, float(VEL[d][c]), v)
        vel.append(v)
    six_w = jnp.where(dirs > 6, 6.0 * WT[7], 6.0 * WT[1])

    bodies = bb_ref[0, 0]
    iota_b = lax.broadcasted_iota(jnp.int32, (body_own, slots), 0)

    def pick(o):
        picks[o] = jnp.where(iota_b == bodies - o * body_own, 1.0, 0.0).astype(BF16)

    loop(0, owners, pick)

    def gather(o, acc):
        p, _ = peer_of(o)
        motion_copy(o, p).wait_recv()
        return acc + dot(stacked(motion_all[p]), picks[p], 1, 0)

    slot_motion = unstacked(
        lax.fori_loop(1, owners, gather, dot(stacked(motion_all[me]), picks[me], 1, 0), unroll=unroll)
    )
    m = unstacked(dot(stacked(slot_motion), slot_t, 1, 0))
    mv = [m[i : i + 1, :] for i in range(6)]
    arm = [larm[i, 0, 0] for i in range(3)]
    wall = [
        mv[0] + mv[4] * arm[2] - mv[5] * arm[1],
        mv[1] + mv[5] * arm[0] - mv[3] * arm[2],
        mv[2] + mv[3] * arm[1] - mv[4] * arm[0],
    ]
    drop = six_w * (vel[0] * wall[0] + vel[1] * wall[1] + vel[2] * wall[2])
    bounce = post - drop
    live = jnp.where(dirs > 0, 1.0, 0.0)
    exchanged = (post + bounce) * live
    force = [vel[c] * exchanged for c in range(3)]
    torque = [
        arm[1] * force[2] - arm[2] * force[1],
        arm[2] * force[0] - arm[0] * force[2],
        arm[0] * force[1] - arm[1] * force[0],
    ]
    loads = jnp.concatenate(force + torque + [jnp.zeros((2, links), F32)], 0)
    slot_load = unstacked(dot(stacked(loads), slot_t, 1, 1))
    slot_parts = stacked(slot_load)

    def spread(o):
        tiles[o] = unstacked(dot(slot_parts, picks[o], 1, 1))

    loop(0, owners, spread)

    here = a * ngz + e

    def force_plane(k, z, slot):
        x, w = plane_dev(k, z)
        return pltpu.make_async_remote_copy(
            src_ref=tiles.at[pl.ds(x * ngy + w * hb, hb)], dst_ref=plane_in.at[slot],
            send_sem=fs.at[k * ngz + z], recv_sem=fr.at[slot],
            device_id=dev(x, b, w), device_id_type=pl.DeviceIdType.MESH,
        )

    for k, z in reversed(plane):
        force_plane(k, z, here).start()
    for k in range(hb):
        plane_in[here, k] = tiles[a * ngy + e * hb + k]

    wm = None
    for part in split3(drop):
        t = dot(row_t, jnp.where(lane_mask, part, 0.0).astype(BF16), 1, 1)
        wm = t if wm is None else wm + t
    wmap[...] = wm

    for c in halo:
        c.wait_recv()
    lane_c = lax.broadcasted_iota(jnp.int32, (8, cells), 1)
    z_c = lane_c - (lane_c // span_z) * span_z
    sub_c = lax.broadcasted_iota(jnp.int32, (8, cells), 0)
    both = []
    for s in range(2):
        t0, t1, t2, t3 = (yin[s, k] for k in range(4))
        out = t0
        for j, d in enumerate(YD[s]):
            cx, _, cz = VEL[d]
            if cx == 1:
                v = jnp.where(lane_c < span_z, pltpu.roll(t1, span_z, 1), pltpu.roll(t0, span_z, 1))
            elif cx == -1:
                v = jnp.where(
                    lane_c >= cells - span_z,
                    pltpu.roll(t2, cells - span_z, 1),
                    pltpu.roll(t0, cells - span_z, 1),
                )
            elif cz == 1:
                v = jnp.where(z_c == 0, pltpu.roll(t3, cells - span_z + 1, 1), pltpu.roll(t0, 1, 1))
            elif cz == -1:
                v = jnp.where(
                    z_c == span_z - 1, pltpu.roll(t3, span_z - 1, 1), pltpu.roll(t0, cells - 1, 1)
                )
            else:
                continue
            out = jnp.where(sub_c == j, v, out)
        both.append(out)
    both.append(jnp.zeros((span_y - 16, cells), F32))
    ycols[...] = jnp.concatenate(both, 0).T

    iz = lax.broadcasted_iota(jnp.int32, (span_z, span_y), 0)
    iy = lax.broadcasted_iota(jnp.int32, (span_z, span_y), 1)

    def stream(x):
        rows = slice(x * span_z, (x + 1) * span_z)
        dm_x = dmap[rows, :]
        wm_x = wmap[rows, :]
        for i in range(19):
            cx, cy, cz = VEL[i]
            sx = x - cx
            inside = 0 <= sx < span_x
            if inside:
                v = relaxed[i, sx * span_z : (sx + 1) * span_z, :]
            else:
                s = 0 if cx > 0 else 1
                v = xin[s, XD[s].index(i)]
            if cz:
                s = 0 if cz > 0 else 1
                if inside:
                    edge = zin[s, ZD[s].index(i), sx : sx + 1, :]
                else:
                    sxx = 0 if cx > 0 else 1
                    j = XZD[sxx].index(i)
                    edge = ein[sxx, j : j + 1, :]
                v = pltpu.roll(v, 1 if cz > 0 else span_z - 1, 0)
                v = jnp.where(iz == (0 if cz > 0 else span_z - 1), edge, v)
            if cy:
                s = 0 if cy > 0 else 1
                j = 8 * s + YD[s].index(i)
                v = pltpu.roll(v, 1 if cy > 0 else span_y - 1, 1)
                v = jnp.where(iy == (0 if cy > 0 else span_y - 1), ycols[rows, j : j + 1], v)
            if i:
                d = OPP[i]
                v = jnp.where(dm_x == float(d), relaxed[d, rows, :] - wm_x, v)
            nxt[i, x] = v

    for x in range(span_x // 2):
        stream(x)

    for k, z in plane:
        x, w = plane_dev(k, z)
        force_plane(k, z, x * ngz + w).wait_recv()
    total = plane_in[0]
    for k in range(1, ngx * ngz):
        total = total + plane_in[k]
    plane_sum[...] = total

    def force_line(k, z, src_b):
        return pltpu.make_async_remote_copy(
            src_ref=plane_sum.at[k], dst_ref=line_in.at[src_b],
            send_sem=cs.at[k * ngz + z], recv_sem=cr.at[src_b],
            device_id=dev(a, e * hb + k, z), device_id_type=pl.DeviceIdType.MESH,
        )

    for k in range(hb):
        for z in range(ngz):
            mine = (e * hb + k == b) & (e == z)

            @pl.when(jnp.logical_not(mine))
            def _():
                force_line(k, z, b).start()

            @pl.when(mine)
            def _():
                line_in[b] = plane_sum[k]

    for x in range(span_x // 2, span_x):
        stream(x)

    loop(1, owners, lambda o: motion_copy(o, me).wait_send())
    for k, z in plane:
        force_plane(k, z, here).wait_send()
    for c in halo:
        c.wait_send()
    for src in range(ngy):
        local = (b // hb == e) & (b == src)

        @pl.when(jnp.logical_not(local))
        def _():
            force_line(0, 0, src).wait_recv()

    load = line_in[0]
    for k in range(1, ngy):
        load = load + line_in[k]
    for k in range(hb):
        for z in range(ngz):
            mine = (e * hb + k == b) & (e == z)

            @pl.when(jnp.logical_not(mine))
            def _():
                force_line(k, z, b).wait_send()

    f = [load[i : i + 1, :] for i in range(6)]
    pos = [bpos[i : i + 1, :] for i in range(3)]
    qw, qx, qy, qz = (bquat[i : i + 1, :] for i in range(4))
    velo = [bvel[i : i + 1, :] + imass[...] * f[i] for i in range(3)]
    velo[2] = velo[2] - GRAV
    rot = [
        [1.0 - 2.0 * (qy * qy + qz * qz), 2.0 * (qx * qy - qw * qz), 2.0 * (qx * qz + qw * qy)],
        [2.0 * (qx * qy + qw * qz), 1.0 - 2.0 * (qx * qx + qz * qz), 2.0 * (qy * qz - qw * qx)],
        [2.0 * (qx * qz - qw * qy), 2.0 * (qy * qz + qw * qx), 1.0 - 2.0 * (qx * qx + qy * qy)],
    ]
    tq = f[3:6]
    acc = [
        iinert[c : c + 1, :] * (rot[0][c] * tq[0] + rot[1][c] * tq[1] + rot[2][c] * tq[2])
        for c in range(3)
    ]
    spin = [
        bspin[r : r + 1, :] + (rot[r][0] * acc[0] + rot[r][1] * acc[1] + rot[r][2] * acc[2])
        for r in range(3)
    ]
    sx, sy, sz = spin
    dq = [
        -(sx * qx + sy * qy + sz * qz),
        sx * qw + sy * qz - sz * qy,
        sy * qw + sz * qx - sx * qz,
        sz * qw + sx * qy - sy * qx,
    ]
    scale = lax.rsqrt(1.0 + 0.25 * (sx * sx + sy * sy + sz * sz))
    quat = [(q + 0.5 * k) * scale for q, k in zip((qw, qx, qy, qz), dq)]
    result = [pos[i] + velo[i] for i in range(3)] + quat + velo + spin
    for i, v in enumerate(result):
        bnext[i : i + 1, :] = v


def write_out(a, b, a_out, b_out, sems):
    copies = [pltpu.make_async_copy(a, a_out, sems.at[0]), pltpu.make_async_copy(b, b_out, sems.at[1])]
    for c in copies:
        c.start()
    for c in copies:
        c.wait()


def shards(sizes, *args):
    pop = args[0]
    span_x, span_z, span_y = pop.shape[1:]
    cells = span_x * span_z
    body_own = args[6].shape[1]
    ngx, ngy, ngz = sizes
    owners = ngx * ngy
    args = list(args)
    args[10] = args[10].reshape(1, -1)
    vm = pl.BlockSpec(memory_space=pltpu.VMEM)
    dma = pltpu.SemaphoreType.DMA
    V = lambda *s: pltpu.VMEM(s, F32)
    args = [pltpu.with_memory_space_constraint(v, pltpu.MemorySpace.HBM) for v in args]
    hbm = pl.BlockSpec(memory_space=pltpu.MemorySpace.HBM)
    outs = pl.pallas_call(
        functools.partial(kernel, sizes),
        out_shape=(
            jax.ShapeDtypeStruct(pop.shape, F32),
            jax.ShapeDtypeStruct((13, body_own), F32),
        ),
        in_specs=[hbm] * len(args),
        out_specs=(vm, vm),
        scratch_shapes=[
            *[pltpu.VMEM(v.shape, v.dtype) for v in args],
            V(19, cells, span_y),
            V(2, 5, span_z, span_y), V(2, 5, span_z, span_y),
            V(2, 5, span_x, span_y), V(2, 5, span_x, span_y),
            V(2, 8, span_y), V(2, 8, span_y),
            V(2, 8, cells), V(2, 4, 8, cells),
            V(16, cells), V(cells, span_y),
            V(cells, span_y), V(cells, span_y),
            V(8, body_own), V(owners, 8, body_own),
            V(owners, 8, body_own), V(ngx * ngz, ngy // ngz, 8, body_own),
            V(ngy // ngz, 8, body_own), V(ngy, 8, body_own),
            pltpu.VMEM((owners, body_own, args[5].shape[-1]), BF16),
            dma((13,)), dma((13,)),
            dma((owners,)), dma((owners,)),
            dma((ngx * ngz,)), dma((ngx * ngz,)),
            dma((ngy,)), dma((ngy,)),
            dma((POP_CHUNKS,)), dma((11,)),
        ],
        compiler_params=pltpu.CompilerParams(
            collective_id=0, has_side_effects=True, vmem_limit_bytes=K1_VMEM
        ),
        name="lattice_step",
    )(*args)
    return pl.pallas_call(
        write_out,
        out_shape=tuple(jax.ShapeDtypeStruct(v.shape, F32) for v in outs),
        in_specs=[vm, vm],
        out_specs=(hbm, hbm),
        scratch_shapes=[dma((2,))],
        compiler_params=pltpu.CompilerParams(vmem_limit_bytes=K2_VMEM),
        name="write_out",
    )(*outs)


def solution(mesh):
    sizes = (mesh.shape["gx"], mesh.shape["gy"], mesh.shape["gz"])
    link = P("gx", "gz", "gy", None)
    body = P(None, ("gx", "gy"))
    return jax.shard_map(
        functools.partial(shards, sizes),
        mesh=mesh,
        in_specs=(
            P(None, "gx", "gz", "gy"), link, link, link, P(None, "gx", "gz", "gy", None), link,
            body, body, body, body, P(("gx", "gy")), body,
        ),
        out_specs=(P(None, "gx", "gz", "gy"), body),
        check_vma=False,
    )
```

```python
import functools

import jax
import jax.numpy as jnp
import numpy as np
from jax import lax
from jax.experimental import pallas as pl
from jax.experimental.pallas import tpu as pltpu
from jax.sharding import PartitionSpec as P

VEL = [
    (0, 0, 0), (1, 0, 0), (-1, 0, 0), (0, 1, 0), (0, -1, 0), (0, 0, 1), (0, 0, -1),
    (1, 1, 0), (-1, -1, 0), (1, -1, 0), (-1, 1, 0), (1, 0, 1), (-1, 0, -1), (1, 0, -1),
    (-1, 0, 1), (0, 1, 1), (0, -1, -1), (0, 1, -1), (0, -1, 1),
]
WT = [1.0 / 3.0] + [1.0 / 18.0] * 6 + [1.0 / 36.0] * 12
OPP = [0, 2, 1, 4, 3, 6, 5, 8, 7, 10, 9, 12, 11, 14, 13, 16, 15, 18, 17]
OMEGA = 1.25
POP_CHUNKS = 2
K1_VMEM = 48 * 1024 * 1024
K2_VMEM = 1024 * 1024
GRAV = 0.02
F32 = jnp.float32
BF16 = jnp.bfloat16


def dirs_of(comp, sign):
    return [d for d in range(19) if VEL[d][comp] == sign]


XD = (dirs_of(0, 1), dirs_of(0, -1))
YD = (dirs_of(1, 1), dirs_of(1, -1))
ZD = (dirs_of(2, 1), dirs_of(2, -1))
XZD = tuple([d for d in XD[s] if VEL[d][2] != 0] for s in range(2))


def split3(v):
    hi = v.astype(BF16).astype(F32)
    rest = v - hi
    mid = rest.astype(BF16).astype(F32)
    return hi, mid, rest - mid


def dot(a, b, ca, cb):
    return lax.dot_general(a, b, (((ca,), (cb,)), ((), ())), preferred_element_type=F32)


def stacked(v):
    return jnp.concatenate(split3(v), 0).astype(BF16)


def unstacked(v):
    k = v.shape[0] // 3
    return v[0:k] + v[k : 2 * k] + v[2 * k : 3 * k]


def kernel(
    sizes,
    pop_h, *rest,
):
    small_h, (nxt, bnext, pop), rest = rest[:11], rest[11:14], rest[14:]
    small, rest = rest[:11], rest[11:]
    step(sizes, pop_h, small_h, pop, *small, nxt, bnext, *rest)


def step(
    sizes, pop_h, small_h,
    pop, lcell, ldir, lslot, larm, bb_ref, bpos, bquat, bvel, bspin, imass, iinert,
    nxt, bnext,
    relaxed, sendx, xin, sendz, zin, sende, ein, sendy, yin, yflat, ycols,
    dmap, wmap, motion_own, motion_all, tiles, plane_in, plane_sum, line_in, picks,
    hs, hr, ms, mr, fs, fr, cs, cr, ps, ss,
):
    ngx, ngy, ngz = sizes
    hb = ngy // ngz
    owners = ngx * ngy
    span_x, span_z, span_y = pop.shape[1:]
    cells = span_x * span_z
    links = lcell.shape[-1]
    body_own = bvel.shape[1]
    slots = bb_ref.shape[-1]
    a, b, e = lax.axis_index("gx"), lax.axis_index("gy"), lax.axis_index("gz")
    me = a * ngy + b
    ap, am = lax.rem(a + 1, ngx), lax.rem(a + ngx - 1, ngx)
    bp, bm = lax.rem(b + 1, ngy), lax.rem(b + ngy - 1, ngy)
    oe = 1 - e

    def dev(x, y, z):
        return {"gx": x, "gy": y, "gz": z}

    def peer_of(offset):
        p = lax.rem(me + offset, owners)
        return p, dev(p // ngy, lax.rem(p, ngy), e)

    def step_of(index, count, k):
        if count & (count - 1) == 0:
            return jnp.bitwise_xor(index, k)
        return lax.rem(index + k, count)

    plane = [(k, z) for k in range(ngx) for z in range(ngz) if k or z]
    line = list(range(1, ngy))

    def plane_dev(k, z):
        return step_of(a, ngx, k), step_of(e, ngz, z)

    unroll = owners <= 16

    def loop(lo, hi, body):
        if unroll:
            for i in range(lo, hi):
                body(i)
        else:
            pl.loop(lo, hi)(body)

    barrier = pltpu.get_barrier_semaphore()

    def greet(o):
        pl.semaphore_signal(barrier, inc=1, device_id=peer_of(o)[1], device_id_type=pl.DeviceIdType.MESH)

    loop(1, owners, greet)
    others = [dev(step_of(a, ngx, k), b, oe) for k in range(ngx)]
    others += [dev(a, step_of(b, ngy, k), oe) for k in line]
    for t in others:
        pl.semaphore_signal(barrier, inc=1, device_id=t, device_id_type=pl.DeviceIdType.MESH)

    small = (lcell, ldir, lslot, larm, bb_ref, bpos, bquat, bvel, bspin, imass, iinert)
    small_in = [
        pltpu.make_async_copy(src, dst, ss.at[k]) for k, (src, dst) in enumerate(zip(small_h, small))
    ]
    chunk = span_x // POP_CHUNKS
    pop_in = [
        pltpu.make_async_copy(
            pop_h.at[:, pl.ds(k * chunk, chunk)], pop.at[:, pl.ds(k * chunk, chunk)], ps.at[k]
        )
        for k in range(POP_CHUNKS)
    ]
    for k in (7, 8):
        small_in[k].start()
    for c in pop_in:
        c.start()
    for k in (0, 1, 2, 3, 4, 5, 6, 9, 10):
        small_in[k].start()

    small_in[7].wait()
    small_in[8].wait()
    motion_own[...] = jnp.concatenate(
        [bvel[...], bspin[...], jnp.zeros((2, body_own), F32)], 0
    )
    motion_all[me] = motion_own[...]

    for x in range(span_x):
        if x % chunk == 0:
            pop_in[x // chunk].wait()
        for z in range(0, span_z, 8):
            f = [pop[d, x, z : z + 8, :] for d in range(19)]
            rho = f[0]
            for d in range(1, 19):
                rho = rho + f[d]
            inv = 1.0 / rho
            u = []
            for c in range(3):
                pos, neg = dirs_of(c, 1), dirs_of(c, -1)
                tot = f[pos[0]] - f[neg[0]]
                for p, q in zip(pos[1:], neg[1:]):
                    tot = tot + (f[p] - f[q])
                u.append(tot * inv)
            usq = 1.0 - 1.5 * (u[0] * u[0] + u[1] * u[1] + u[2] * u[2])
            rows = pl.ds(x * span_z + z, 8)
            keep = 1.0 - OMEGA
            relaxed[0, rows, :] = keep * f[0] + (OMEGA * WT[0]) * rho * usq
            for d in range(1, 19, 2):
                terms = [u[c] if VEL[d][c] > 0 else -u[c] for c in range(3) if VEL[d][c]]
                proj = terms[0] if len(terms) == 1 else terms[0] + terms[1]
                scale = (OMEGA * WT[d]) * rho
                even = scale * (usq + 4.5 * proj * proj)
                odd = scale * (3.0 * proj)
                relaxed[d, rows, :] = keep * f[d] + (even + odd)
                relaxed[d + 1, rows, :] = keep * f[d + 1] + (even - odd)

    for s in range(2):
        xe = (span_x - 1) if s == 0 else 0
        ze = (span_z - 1) if s == 0 else 0
        for j, d in enumerate(XD[s]):
            sendx[s, j] = relaxed[d, xe * span_z : (xe + 1) * span_z, :]
        for j, d in enumerate(ZD[s]):
            for x in range(span_x):
                r = x * span_z + ze
                sendz[s, j, x : x + 1, :] = relaxed[d, r : r + 1, :]
        sende[s] = jnp.zeros(sende.shape[1:], F32)
        for j, d in enumerate(XZD[s]):
            r = xe * span_z + ((span_z - 1) if VEL[d][2] > 0 else 0)
            sende[s, j : j + 1, :] = relaxed[d, r : r + 1, :]
    lane = lax.broadcasted_iota(jnp.int32, (cells, span_y), 1)
    pack = jnp.zeros((cells, span_y), F32)
    for s in range(2):
        ye = (span_y - 1) if s == 0 else 0
        for j, d in enumerate(YD[s]):
            pack = jnp.where(lane == 8 * s + j, relaxed[d, :, ye : ye + 1], pack)
    pack_t = pack.T
    for s in range(2):
        sendy[s] = pack_t[8 * s : 8 * s + 8, :]

    pl.semaphore_wait(barrier, owners - 1 + len(others))

    def motion_copy(o, slot):
        return pltpu.make_async_remote_copy(
            src_ref=motion_own, dst_ref=motion_all.at[slot], send_sem=ms.at[o], recv_sem=mr.at[slot],
            device_id=peer_of(o)[1], device_id_type=pl.DeviceIdType.MESH,
        )

    loop(1, owners, lambda o: motion_copy(o, me).start())

    halo = []

    def rim(src, dst, target):
        k = len(halo)
        c = pltpu.make_async_remote_copy(
            src_ref=src, dst_ref=dst, send_sem=hs.at[k], recv_sem=hr.at[k],
            device_id=target, device_id_type=pl.DeviceIdType.MESH,
        )
        c.start()
        halo.append(c)

    for s in range(2):
        xt, yt = (ap, bp) if s == 0 else (am, bm)
        rim(sendx.at[s], xin.at[s], dev(xt, b, e))
        rim(sende.at[s], ein.at[s], dev(xt, b, oe))
        rim(sendy.at[s], yin.at[s, 0], dev(a, yt, e))
        rim(sendy.at[s], yin.at[s, 1], dev(ap, yt, e))
        rim(sendy.at[s], yin.at[s, 2], dev(am, yt, e))
        rim(sendy.at[s], yin.at[s, 3], dev(a, yt, oe))
    rim(sendz, zin, dev(a, b, oe))

    for k in (0, 1, 2, 3, 4, 5, 6, 9, 10):
        small_in[k].wait()

    cell = lcell[0, 0]
    dirs = ldir[0, 0]
    row_of = cell // span_y
    lane_of = cell - row_of * span_y
    dirs_f = dirs.astype(F32)
    iota_c = lax.broadcasted_iota(jnp.int32, (cells, links), 0)
    iota_y = lax.broadcasted_iota(jnp.int32, (span_y, links), 0)
    row_t = jnp.where(iota_c == row_of, 1.0, 0.0).astype(BF16)
    lane_mask = iota_y == lane_of
    dmap[...] = dot(row_t, jnp.where(lane_mask, dirs_f, 0.0).astype(BF16), 1, 1)
    dm = dmap[...]
    post_map = jnp.zeros((cells, span_y), F32)
    for d in range(1, 19):
        post_map = jnp.where(dm == float(d), relaxed[d], post_map)
    picked = None
    for part in split3(post_map):
        t = dot(part.astype(BF16), row_t, 0, 0)
        picked = t if picked is None else picked + t
    post = jnp.sum(jnp.where(lane_mask, picked, 0.0), axis=0, keepdims=True)
    iota_s = lax.broadcasted_iota(jnp.int32, (slots, links), 0)
    slot_t = jnp.where(iota_s == lslot[0, 0], 1.0, 0.0).astype(BF16)

    vel = []
    for c in range(3):
        v = jnp.zeros((1, links), F32)
        for d in range(1, 19):
            if VEL[d][c]:
                v = jnp.where(dirs == d, float(VEL[d][c]), v)
        vel.append(v)
    six_w = jnp.where(dirs > 6, 6.0 * WT[7], 6.0 * WT[1])

    bodies = bb_ref[0, 0]
    iota_b = lax.broadcasted_iota(jnp.int32, (body_own, slots), 0)

    def pick(o):
        picks[o] = jnp.where(iota_b == bodies - o * body_own, 1.0, 0.0).astype(BF16)

    loop(0, owners, pick)

    def gather(o, acc):
        return acc + dot(stacked(motion_all[o]), picks[o], 1, 0)

    loop(1, owners, lambda o: motion_copy(o, peer_of(o)[0]).wait_recv())
    slot_motion = unstacked(
        lax.fori_loop(0, owners, gather, jnp.zeros((24, slots), F32), unroll=unroll)
    )
    m = unstacked(dot(stacked(slot_motion), slot_t, 1, 0))
    mv = [m[i : i + 1, :] for i in range(6)]
    arm = [larm[i, 0, 0] for i in range(3)]
    wall = [
        mv[0] + mv[4] * arm[2] - mv[5] * arm[1],
        mv[1] + mv[5] * arm[0] - mv[3] * arm[2],
        mv[2] + mv[3] * arm[1] - mv[4] * arm[0],
    ]
    drop = six_w * (vel[0] * wall[0] + vel[1] * wall[1] + vel[2] * wall[2])
    bounce = post - drop
    live = jnp.where(dirs > 0, 1.0, 0.0)
    exchanged = (post + bounce) * live
    force = [vel[c] * exchanged for c in range(3)]
    torque = [
        arm[1] * force[2] - arm[2] * force[1],
        arm[2] * force[0] - arm[0] * force[2],
        arm[0] * force[1] - arm[1] * force[0],
    ]
    loads = jnp.concatenate(force + torque + [jnp.zeros((2, links), F32)], 0)
    slot_load = unstacked(dot(stacked(loads), slot_t, 1, 1))
    slot_parts = stacked(slot_load)

    def spread(o):
        tiles[o] = unstacked(dot(slot_parts, picks[o], 1, 1))

    loop(0, owners, spread)

    here = a * ngz + e

    def force_plane(k, z, slot):
        x, w = plane_dev(k, z)
        return pltpu.make_async_remote_copy(
            src_ref=tiles.at[pl.ds(x * ngy + w * hb, hb)], dst_ref=plane_in.at[slot],
            send_sem=fs.at[k * ngz + z], recv_sem=fr.at[slot],
            device_id=dev(x, b, w), device_id_type=pl.DeviceIdType.MESH,
        )

    for k, z in reversed(plane):
        force_plane(k, z, here).start()
    for k in range(hb):
        plane_in[here, k] = tiles[a * ngy + e * hb + k]

    wm = None
    for part in split3(drop):
        t = dot(row_t, jnp.where(lane_mask, part, 0.0).astype(BF16), 1, 1)
        wm = t if wm is None else wm + t
    wmap[...] = wm

    for c in halo:
        c.wait_recv()
    lane_c = lax.broadcasted_iota(jnp.int32, (8, cells), 1)
    z_c = lane_c - (lane_c // span_z) * span_z
    sub_c = lax.broadcasted_iota(jnp.int32, (8, cells), 0)
    both = []
    for s in range(2):
        t0, t1, t2, t3 = (yin[s, k] for k in range(4))
        out = t0
        for j, d in enumerate(YD[s]):
            cx, _, cz = VEL[d]
            if cx == 1:
                v = jnp.where(lane_c < span_z, pltpu.roll(t1, span_z, 1), pltpu.roll(t0, span_z, 1))
            elif cx == -1:
                v = jnp.where(
                    lane_c >= cells - span_z,
                    pltpu.roll(t2, cells - span_z, 1),
                    pltpu.roll(t0, cells - span_z, 1),
                )
            elif cz == 1:
                v = jnp.where(z_c == 0, pltpu.roll(t3, cells - span_z + 1, 1), pltpu.roll(t0, 1, 1))
            elif cz == -1:
                v = jnp.where(
                    z_c == span_z - 1, pltpu.roll(t3, span_z - 1, 1), pltpu.roll(t0, cells - 1, 1)
                )
            else:
                continue
            out = jnp.where(sub_c == j, v, out)
        both.append(out)
    both.append(jnp.zeros((span_y - 16, cells), F32))
    ycols[...] = jnp.concatenate(both, 0).T

    iz = lax.broadcasted_iota(jnp.int32, (span_z, span_y), 0)
    iy = lax.broadcasted_iota(jnp.int32, (span_z, span_y), 1)

    def stream(x):
        rows = slice(x * span_z, (x + 1) * span_z)
        dm_x = dmap[rows, :]
        wm_x = wmap[rows, :]
        for i in range(19):
            cx, cy, cz = VEL[i]
            sx = x - cx
            inside = 0 <= sx < span_x
            if inside:
                v = relaxed[i, sx * span_z : (sx + 1) * span_z, :]
            else:
                s = 0 if cx > 0 else 1
                v = xin[s, XD[s].index(i)]
            if cz:
                s = 0 if cz > 0 else 1
                if inside:
                    edge = zin[s, ZD[s].index(i), sx : sx + 1, :]
                else:
                    sxx = 0 if cx > 0 else 1
                    j = XZD[sxx].index(i)
                    edge = ein[sxx, j : j + 1, :]
                v = pltpu.roll(v, 1 if cz > 0 else span_z - 1, 0)
                v = jnp.where(iz == (0 if cz > 0 else span_z - 1), edge, v)
            if cy:
                s = 0 if cy > 0 else 1
                j = 8 * s + YD[s].index(i)
                v = pltpu.roll(v, 1 if cy > 0 else span_y - 1, 1)
                v = jnp.where(iy == (0 if cy > 0 else span_y - 1), ycols[rows, j : j + 1], v)
            if i:
                d = OPP[i]
                v = jnp.where(dm_x == float(d), relaxed[d, rows, :] - wm_x, v)
            nxt[i, x] = v

    for x in range(span_x // 2):
        stream(x)

    for k, z in plane:
        x, w = plane_dev(k, z)
        force_plane(k, z, x * ngz + w).wait_recv()
    total = plane_in[0]
    for k in range(1, ngx * ngz):
        total = total + plane_in[k]
    plane_sum[...] = total

    def force_line(k, z, src_b):
        return pltpu.make_async_remote_copy(
            src_ref=plane_sum.at[k], dst_ref=line_in.at[src_b],
            send_sem=cs.at[k * ngz + z], recv_sem=cr.at[src_b],
            device_id=dev(a, e * hb + k, z), device_id_type=pl.DeviceIdType.MESH,
        )

    for k in range(hb):
        for z in range(ngz):
            mine = (e * hb + k == b) & (e == z)

            @pl.when(jnp.logical_not(mine))
            def _():
                force_line(k, z, b).start()

            @pl.when(mine)
            def _():
                line_in[b] = plane_sum[k]

    for x in range(span_x // 2, span_x):
        stream(x)

    loop(1, owners, lambda o: motion_copy(o, me).wait_send())
    for k, z in plane:
        force_plane(k, z, here).wait_send()
    for c in halo:
        c.wait_send()
    for src in range(ngy):
        local = (b // hb == e) & (b == src)

        @pl.when(jnp.logical_not(local))
        def _():
            force_line(0, 0, src).wait_recv()

    load = line_in[0]
    for k in range(1, ngy):
        load = load + line_in[k]
    for k in range(hb):
        for z in range(ngz):
            mine = (e * hb + k == b) & (e == z)

            @pl.when(jnp.logical_not(mine))
            def _():
                force_line(k, z, b).wait_send()

    f = [load[i : i + 1, :] for i in range(6)]
    pos = [bpos[i : i + 1, :] for i in range(3)]
    qw, qx, qy, qz = (bquat[i : i + 1, :] for i in range(4))
    velo = [bvel[i : i + 1, :] + imass[...] * f[i] for i in range(3)]
    velo[2] = velo[2] - GRAV
    rot = [
        [1.0 - 2.0 * (qy * qy + qz * qz), 2.0 * (qx * qy - qw * qz), 2.0 * (qx * qz + qw * qy)],
        [2.0 * (qx * qy + qw * qz), 1.0 - 2.0 * (qx * qx + qz * qz), 2.0 * (qy * qz - qw * qx)],
        [2.0 * (qx * qz - qw * qy), 2.0 * (qy * qz + qw * qx), 1.0 - 2.0 * (qx * qx + qy * qy)],
    ]
    tq = f[3:6]
    acc = [
        iinert[c : c + 1, :] * (rot[0][c] * tq[0] + rot[1][c] * tq[1] + rot[2][c] * tq[2])
        for c in range(3)
    ]
    spin = [
        bspin[r : r + 1, :] + (rot[r][0] * acc[0] + rot[r][1] * acc[1] + rot[r][2] * acc[2])
        for r in range(3)
    ]
    sx, sy, sz = spin
    dq = [
        -(sx * qx + sy * qy + sz * qz),
        sx * qw + sy * qz - sz * qy,
        sy * qw + sz * qx - sx * qz,
        sz * qw + sx * qy - sy * qx,
    ]
    scale = lax.rsqrt(1.0 + 0.25 * (sx * sx + sy * sy + sz * sz))
    quat = [(q + 0.5 * k) * scale for q, k in zip((qw, qx, qy, qz), dq)]
    result = [pos[i] + velo[i] for i in range(3)] + quat + velo + spin
    for i, v in enumerate(result):
        bnext[i : i + 1, :] = v


def write_out(a, b, a_out, b_out, sems):
    copies = [pltpu.make_async_copy(a, a_out, sems.at[0]), pltpu.make_async_copy(b, b_out, sems.at[1])]
    for c in copies:
        c.start()
    for c in copies:
        c.wait()


def shards(sizes, *args):
    pop = args[0]
    span_x, span_z, span_y = pop.shape[1:]
    cells = span_x * span_z
    body_own = args[6].shape[1]
    ngx, ngy, ngz = sizes
    owners = ngx * ngy
    args = list(args)
    args[10] = args[10].reshape(1, -1)
    vm = pl.BlockSpec(memory_space=pltpu.VMEM)
    dma = pltpu.SemaphoreType.DMA
    V = lambda *s: pltpu.VMEM(s, F32)
    args = [pltpu.with_memory_space_constraint(v, pltpu.MemorySpace.HBM) for v in args]
    hbm = pl.BlockSpec(memory_space=pltpu.MemorySpace.HBM)
    outs = pl.pallas_call(
        functools.partial(kernel, sizes),
        out_shape=(
            jax.ShapeDtypeStruct(pop.shape, F32),
            jax.ShapeDtypeStruct((13, body_own), F32),
        ),
        in_specs=[hbm] * len(args),
        out_specs=(vm, vm),
        scratch_shapes=[
            *[pltpu.VMEM(v.shape, v.dtype) for v in args],
            V(19, cells, span_y),
            V(2, 5, span_z, span_y), V(2, 5, span_z, span_y),
            V(2, 5, span_x, span_y), V(2, 5, span_x, span_y),
            V(2, 8, span_y), V(2, 8, span_y),
            V(2, 8, cells), V(2, 4, 8, cells),
            V(16, cells), V(cells, span_y),
            V(cells, span_y), V(cells, span_y),
            V(8, body_own), V(owners, 8, body_own),
            V(owners, 8, body_own), V(ngx * ngz, ngy // ngz, 8, body_own),
            V(ngy // ngz, 8, body_own), V(ngy, 8, body_own),
            pltpu.VMEM((owners, body_own, args[5].shape[-1]), BF16),
            dma((13,)), dma((13,)),
            dma((owners,)), dma((owners,)),
            dma((ngx * ngz,)), dma((ngx * ngz,)),
            dma((ngy,)), dma((ngy,)),
            dma((POP_CHUNKS,)), dma((11,)),
        ],
        compiler_params=pltpu.CompilerParams(
            collective_id=0, has_side_effects=True, vmem_limit_bytes=K1_VMEM
        ),
        name="lattice_step",
    )(*args)
    return pl.pallas_call(
        write_out,
        out_shape=tuple(jax.ShapeDtypeStruct(v.shape, F32) for v in outs),
        in_specs=[vm, vm],
        out_specs=(hbm, hbm),
        scratch_shapes=[dma((2,))],
        compiler_params=pltpu.CompilerParams(vmem_limit_bytes=K2_VMEM),
        name="write_out",
    )(*outs)


def solution(mesh):
    sizes = (mesh.shape["gx"], mesh.shape["gy"], mesh.shape["gz"])
    link = P("gx", "gz", "gy", None)
    body = P(None, ("gx", "gy"))
    return jax.shard_map(
        functools.partial(shards, sizes),
        mesh=mesh,
        in_specs=(
            P(None, "gx", "gz", "gy"), link, link, link, P(None, "gx", "gz", "gy", None), link,
            body, body, body, body, P(("gx", "gy")), body,
        ),
        out_specs=(P(None, "gx", "gz", "gy"), body),
        check_vma=False,
    )
```
